512 devices in a mesh: samp: 32 (over y_hi, z), head: 16 (over y_lo, x, core).
Axes of the slice: x: 4, y: 4 (y_hi: 2, y_lo: 2; y = y_hi * 2 + y_lo), z: 16, core: 2. Of those that a mesh axis runs over, the one named last changes fastest.
Arguments:
- queries: bfloat16 [32, 768, 512], P('samp', 'head'), may hold values from -10 to 10
- keys: bfloat16 [32, 768, 512], P('samp', 'head'), may hold values from -10 to 10
- values: bfloat16 [32, 768, 512], P('samp', 'head'), may hold values from -6 to 6
- out_grad: bfloat16 [32, 768, 512], P('samp', 'head'), may hold values from -6 to 6
- pair: bfloat16 [512, 512, 128], P('head', 'samp'), may hold values from -6 to 6
- ln_gain: float32 [128], replicated, may hold values from 0.25 to 1.75
- proj_weight: bfloat16 [128, 16], replicated, may hold values from -0.5 to 0.5
- token_mask: int32 [512], replicated, may hold values from 0 to 1, as said below
- atom_map: int32 [4096], replicated, may hold values from 0 to 511, never falling along the last dimension, each value on 1 to 24 neighbouring positions
Outputs:
- attended: bfloat16 [32, 768, 512], P('samp', 'head')
- query_grad: bfloat16 [32, 768, 512], P('samp', 'head')
- key_grad: bfloat16 [32, 768, 512], P('samp', 'head')
- value_grad: bfloat16 [32, 768, 512], P('samp', 'head')
- pair_grad: bfloat16 [512, 512, 128], P('head', 'samp')
- weight_grad: float32 [128, 16], replicated
- gain_grad: float32 [128], replicated
The draws below stay inside these ranges and needn't reach their ends.
Inputs may be any that keep to these rules, and one draw needn't show every extreme that they name: `token_mask`: real tokens form a prefix of 256 or more tokens; the last token is padding.
All inputs are finite; a program needn't handle non-finite values.
Results may differ from the reference program's by a relative error of at most 0.02.
Values may be sent and summed in bfloat16 or wider, within the bound.
A program may use at most 64 MiB of HBM per device.

```python
import math
import jax
import jax.numpy as jnp
import numpy as np
from jax import lax

N = 512
D = 768
HEADS = 16
D_PAIR = 128
ATOM_MOST = 24
SAMPLES = 32
ATOMS = 4096


def drawn_pair(key):
    base = jax.random.fold_in(key, 11)
    key_query, key_keys = jax.random.split(base, 2)
    shape = (SAMPLES, N, D)
    query_all = jnp.clip(jax.random.normal(key_query, shape, jnp.float32), -6.0, 6.0)
    keys_all = jnp.clip(jax.random.normal(key_keys, shape, jnp.float32), -6.0, 6.0)
    return (jnp.swapaxes(query_all, 1, 2), jnp.swapaxes(keys_all, 1, 2))


def draw_queries(key, part):
    return drawn_pair(key)[0].astype(jnp.bfloat16)


def draw_keys(key, part):
    return drawn_pair(key)[1].astype(jnp.bfloat16)


def draw_token_mask(key, part):
    length = jax.random.randint(jax.random.fold_in(key, 23), (), N // 2, N)
    return (jnp.arange(N) < length).astype(jnp.int32)


def shard_levels(stream_key, shape, cuts, low, top_value):
    def one(dim, shards_of):
        draws = jax.random.uniform(jax.random.fold_in(jax.random.fold_in(stream_key, 6), dim), (shards_of,), jnp.float32, low / len(cuts), top_value / len(cuts))
        return jnp.repeat(jnp.exp(draws), shape[dim] // shards_of).reshape((-1,) + (1,) * (len(shape) - dim - 1))

    loudness = one(*cuts[0])
    for cut in cuts[1:]:
        loudness = loudness * one(*cut)
    return loudness


def split_up(count, total, limit, lean):
    loads = [(1 << 20) // math.isqrt(rank ** lean) + 1 for rank in range(2, count + 1)]
    rest, given = total - limit - (count - 1), [1] * (count - 1)
    while rest > 0:
        movable = [i for i in range(count - 1) if given[i] < limit]
        pool, budget = sum([loads[i] for i in movable]), rest
        for i in movable:
            extra = min(limit - given[i], max(1, budget * loads[i] // pool), rest)
            given[i] = given[i] + extra
            rest = rest - extra
    return np.array([limit] + given)


def ragged(stream_key, number_of, total, reach, slope):
    if number_of == 2:
        one = jax.random.randint(stream_key, (), max(1, total - reach), min(reach, total - 1) + 1)
        return jnp.stack([one, total - one])
    sizes = jnp.asarray(split_up(number_of, total, reach, slope), jnp.int32)
    twos = (number_of - 1) // 2
    donor, taker = sizes[1:1 + 2 * twos:2], sizes[2:2 + 2 * twos:2]
    slack = jnp.minimum(donor - 1, reach - taker)
    moved = jax.random.randint(jax.random.fold_in(stream_key, 1), (twos,), 0, 1 << 20) % (slack + 1)
    sizes = sizes.at[1:1 + 2 * twos:2].set(donor - moved).at[2:2 + 2 * twos:2].set(taker + moved)
    return sizes[jax.random.permutation(jax.random.fold_in(stream_key, 2), number_of)]


def centred(key, extent, deviation, reach, pieces=(), kind=jnp.bfloat16):
    values = deviation * jax.random.normal(key, extent, jnp.float32)
    if pieces:
        values = values * shard_levels(key, extent, pieces, -0.22, 0.18)
    return jnp.clip(values, -reach, reach).astype(kind)


def setup_inputs(seed: int = 0) -> dict:
    seeds = jax.random.split(jax.random.key(seed), 10)
    return {
        "queries": draw_queries(jax.random.fold_in(seeds[9], 71), 0),
        "keys": draw_keys(jax.random.fold_in(seeds[9], 71), 0),
        "values": centred(seeds[2], (SAMPLES, D, N), 1.0, 6.0, ((0, 32), (1, 16))),
        "out_grad": centred(seeds[3], (SAMPLES, D, N), 1.0, 6.0, ((0, 32), (1, 16))),
        "pair": centred(seeds[4], (N, N, D_PAIR), 1.0, 6.0, ((0, 16), (1, 32))),
        "ln_gain": jnp.clip(1.0 + 0.15 * jax.random.normal(seeds[5], (D_PAIR,), jnp.float32), 0.25, 1.75),
        "proj_weight": centred(seeds[6], (D_PAIR, HEADS), D_PAIR ** -0.5, 0.5),
        "token_mask": draw_token_mask(jax.random.fold_in(seeds[9], 71), 0),
        "atom_map": jnp.searchsorted(jnp.cumsum(ragged(seeds[8], N, ATOMS, ATOM_MOST, 2)), jnp.arange(ATOMS), side="right").astype(jnp.int32),
    }


def token_weights(atom_map, token_mask):
    count = token_mask.shape[0]
    ends = jnp.searchsorted(atom_map, jnp.arange(count, dtype=jnp.int32), side='right').astype(jnp.int32)
    starts = jnp.concatenate([jnp.zeros((1,), jnp.int32), ends[:-1]])
    return (ends - starts).astype(jnp.float32) * (count / atom_map.shape[0]) * token_mask.astype(jnp.float32)

def layer_norm(pair, ln_gain):
    wide = pair.astype(jnp.float32)
    center = lax.optimization_barrier(jnp.mean(wide, axis=-1, keepdims=True))
    spread = lax.optimization_barrier(jnp.mean(jnp.square(wide - center), axis=-1, keepdims=True))
    inv_std = 1.0 / jnp.sqrt(spread + 1e-05)
    normed = (wide - center) * inv_std
    lnout = (normed * ln_gain).astype(jnp.bfloat16)
    return (normed, inv_std, lnout)

def attend(query_row, key_row, value_row, grad_row, bias, key_keep, tok_weight):
    count = query_row.shape[1]
    local_heads = bias.shape[0]
    query_h = query_row.reshape(local_heads, -1, count).astype(jnp.float32)
    key_h = key_row.reshape(local_heads, -1, count).astype(jnp.float32)
    value_h = value_row.reshape(local_heads, -1, count).astype(jnp.float32)
    inv_root = 1.0 / jnp.sqrt(jnp.float32(query_h.shape[1]))
    scores = jnp.einsum('hdi,hdj->hij', query_h, key_h) * inv_root + bias.astype(jnp.float32)
    scores = jnp.where(key_keep[None, None, :], scores, jnp.float32(-1000000000.0))
    largest = lax.optimization_barrier(jnp.max(scores, axis=-1, keepdims=True))
    expo = jnp.exp(scores - largest)
    prob = expo / lax.optimization_barrier(jnp.sum(expo, axis=-1, keepdims=True))
    prob_b = prob.astype(jnp.bfloat16).astype(jnp.float32)
    attended = jnp.einsum('hij,hdj->hdi', prob_b, value_h).astype(jnp.bfloat16)
    grad_in = (grad_row.astype(jnp.float32) * tok_weight[None, :]).astype(jnp.bfloat16)
    grad_h = grad_in.reshape(local_heads, -1, count).astype(jnp.float32)
    dprob = jnp.einsum('hdi,hdj->hij', grad_h, value_h)
    row_dot = lax.optimization_barrier(jnp.sum(prob * dprob, axis=-1, keepdims=True))
    dscore = prob * (dprob - row_dot)
    dscore_b = dscore.astype(jnp.bfloat16).astype(jnp.float32)
    query_grad = (jnp.einsum('hij,hdj->hdi', dscore_b, key_h) * inv_root).astype(jnp.bfloat16)
    key_grad = (jnp.einsum('hij,hdi->hdj', dscore_b, query_h) * inv_root).astype(jnp.bfloat16)
    value_grad = jnp.einsum('hij,hdi->hdj', prob_b, grad_h).astype(jnp.bfloat16)
    shape = (-1, count)
    return (attended.reshape(shape), query_grad.reshape(shape), key_grad.reshape(shape), value_grad.reshape(shape), dscore.astype(jnp.float32))

def reference(queries, keys, values, out_grad, pair, ln_gain, proj_weight, token_mask, atom_map):
    count = pair.shape[0]
    key_keep = token_mask > 0
    tok_weight = token_weights(atom_map, token_mask)
    normed, inv_std, lnout = layer_norm(pair, ln_gain)
    bias = jnp.einsum('ijc,ch->hij', lnout.astype(jnp.float32), proj_weight.astype(jnp.float32)).astype(jnp.bfloat16)

    def one_sample(total, items):
        query_row, key_row, value_row, grad_row = items
        attended, query_grad, key_grad, value_grad, dscore = attend(query_row, key_row, value_row, grad_row, bias, key_keep, tok_weight)
        return (total + dscore, (attended, query_grad, key_grad, value_grad))
    start = jnp.zeros(bias.shape, jnp.float32)
    bias_grad, outs = lax.scan(one_sample, start, (queries, keys, values, out_grad))
    attended, query_grad, key_grad, value_grad = outs
    highest = lax.Precision.HIGHEST
    lnout_grad = jnp.einsum('hij,ch->ijc', bias_grad, proj_weight.astype(jnp.float32), precision=highest)
    weight_grad = jnp.einsum('ijc,hij->ch', lnout.astype(jnp.float32), bias_grad, precision=highest) / count
    gain_grad = lax.optimization_barrier(jnp.sum(lnout_grad * normed, axis=(0, 1))) / count
    scaled = lnout_grad * ln_gain
    pair_grad = (scaled - lax.optimization_barrier(jnp.mean(scaled, axis=-1, keepdims=True)) - normed * lax.optimization_barrier(jnp.mean(scaled * normed, axis=-1, keepdims=True))) * inv_std
    return (attended, query_grad, key_grad, value_grad, pair_grad.astype(jnp.bfloat16), weight_grad, gain_grad)
```

```python
import functools
import math

import jax
import jax.numpy as jnp
from jax import lax
from jax.experimental import pallas as pl
from jax.experimental.pallas import tpu as pltpu
from jax.sharding import PartitionSpec as P

MESH = pl.DeviceIdType.MESH
F32 = jnp.float32
BF16 = jnp.bfloat16
LANES = 128
YH = 2


def dot_nn(a, b):
    return lax.dot_general(a, b, (((1,), (0,)), ((), ())), preferred_element_type=F32)


def dot_nt(a, b):
    return lax.dot_general(a, b, (((1,), (1,)), ((), ())), preferred_element_type=F32)


def dot_tn(a, b):
    return lax.dot_general(a, b, (((0,), (0,)), ((), ())), preferred_element_type=F32)


def kernel(
    samp, heads, atoms,
    q_ref, k_ref, v_ref, g_ref, pair_ref, gain_ref, w_ref, mask_ref, atom_ref,
    att_ref, qg_ref, kg_ref, vg_ref, pg_ref, wg_ref, gg_ref,
    xs, norm, inv, ln, tile32, tsend, trecv, bias, score, dprob, probb, dsb, top,
    rin, racc, fin, brecv, part, arr1, row, arr2, tot, res,
    a_send, a_recv, ag_send, ag_recv, rs_send, rs_recv, b_send, b_recv,
    s1, r1, s2, r2, s3, r3,
):
    zn = samp // YH
    hops = zn // 4
    plane = YH * heads
    feat, count = q_ref.shape
    tj, ti = count // samp, count // heads
    groups = LANES // ti
    tiles = count // LANES
    inv_root = 1.0 / math.sqrt(feat)

    me_s, me_h = lax.axis_index("samp"), lax.axis_index("head")
    yh, z = me_s // zn, lax.rem(me_s, zn)
    me_p = yh * heads + me_h
    grp = lax.rem(me_h, groups)

    def at_plane(p):
        return (p // heads) * zn + z, lax.rem(p, heads)

    def wrap(o):
        return lax.rem(z + (o + 2 * zn), zn)

    def at_z(o):
        return yh * zn + wrap(o), me_h

    barrier = pltpu.get_barrier_semaphore()

    def greet(off, c):
        pl.semaphore_signal(barrier, inc=1, device_id=at_plane(lax.rem(me_p + off, plane)), device_id_type=MESH)
        return c

    lax.fori_loop(1, plane, greet, 0)
    for o in (1, -1, 2, -2):
        pl.semaphore_signal(barrier, inc=1, device_id=at_z(o), device_id_type=MESH)

    gain = gain_ref[...]
    xs[...] = pair_ref[...].astype(F32).reshape(ti * tj, LANES)
    for j in range(tj):
        x = xs[pl.ds(j, ti, stride=tj), :]
        mu = jnp.mean(x, axis=-1, keepdims=True)
        d = x - mu
        iv = 1.0 / jnp.sqrt(jnp.mean(d * d, axis=-1, keepdims=True) + 1e-05)
        n = d * iv
        rows = slice(j * ti, (j + 1) * ti)
        norm[rows, :] = n
        inv[rows, :] = jnp.broadcast_to(iv, (ti, LANES))
        ln[rows, :] = (n * gain).astype(BF16)
    wt = w_ref[...]
    zb = dot_nt(wt, ln[...])
    lane_group = lax.broadcasted_iota(jnp.int32, (heads, LANES), 1) // ti
    for j in range(tj):
        t, jj = j // groups, j % groups
        turned = pltpu.roll(zb[:, t * LANES : (t + 1) * LANES], lax.rem(grp - jj + groups, groups) * ti, axis=1)
        tile32[pl.ds(j, heads, stride=tj), :] = jnp.where(lane_group == grp, turned, 0.0)
    tsend[...] = tile32[...].reshape(heads, tj, LANES).astype(BF16)

    pl.semaphore_wait(barrier, plane - 1 + 4)

    def all_of(ref, n, sem):
        return pltpu.make_async_copy(ref.at[pl.ds(0, n)], ref.at[pl.ds(0, n)], sem)

    def plane_send(src_of, dst, send, recv):
        def body(off, c):
            p = lax.rem(me_p + off, plane)
            pltpu.make_async_remote_copy(
                src_ref=src_of(p), dst_ref=dst.at[me_p], send_sem=send, recv_sem=recv,
                device_id=at_plane(p), device_id_type=MESH,
            ).start()
            return c

        lax.fori_loop(1, plane, body, 0)

    plane_send(lambda p: tsend.at[lax.rem(p, heads)], trecv, a_send.at[0], a_recv.at[0])
    trecv[me_p] = tsend[me_h]

    length = jnp.sum(mask_ref[...].astype(F32), axis=(0, 1), keepdims=True)
    step = 64

    def counting(c, carry):
        ids = lax.broadcasted_iota(jnp.int32, (step, LANES), 0) + c * step
        acc = jnp.zeros((step, LANES), F32)
        for r in range(atoms // LANES):
            acc = acc + jnp.where(atom_ref[r : r + 1, :] == ids, 1.0, 0.0)
        xs[pl.ds(pl.multiple_of(c * step, step), step), :] = acc
        return carry

    lax.fori_loop(0, count // step, counting, 0)
    counts = dot_nt(jnp.ones((8, LANES), BF16), xs[0:count, :].astype(BF16))[0:1, :]
    real = lax.broadcasted_iota(jnp.int32, (1, count), 1).astype(F32) < length
    tok = jnp.where(real, counts * (count / atoms), 0.0)
    query, key, value = q_ref[...], k_ref[...], v_ref[...]
    grad = (g_ref[...].astype(F32) * tok).astype(BF16)
    chunk = LANES // tj
    for c in range(tiles):
        cols = slice(c * LANES, (c + 1) * LANES)
        keep = lax.broadcasted_iota(jnp.int32, (LANES, 1), 0).astype(F32) + float(c * LANES) < length
        s = jnp.where(keep, dot_tn(key[:, cols], query) * inv_root, -1000000000.0)
        score[c * chunk : (c + 1) * chunk] = s.reshape(chunk, tj, count)
        dprob[c * chunk : (c + 1) * chunk] = dot_tn(value[:, cols], grad).reshape(chunk, tj, count)
    top[...] = jnp.full(top.shape, -3.0e38, F32)

    all_of(trecv, plane - 1, a_recv.at[0]).wait()
    for y in range(YH):
        for t in range(tiles):
            block = trecv[y * heads + t * groups]
            for u in range(1, groups):
                block = block + trecv[y * heads + t * groups + u]
            bias[y, z, :, t * LANES : (t + 1) * LANES] = block

    def ag_copy(sem, origin, o):
        return pltpu.make_async_remote_copy(
            src_ref=bias.at[:, wrap(origin)], dst_ref=bias.at[:, wrap(origin)],
            send_sem=ag_send.at[sem], recv_sem=ag_recv.at[sem], device_id=at_z(o), device_id_type=MESH,
        )

    def absorb(origin):
        o = wrap(origin)
        best = top[...]
        for y in range(YH):
            s = score[y * zn + o] + bias[y, o].astype(F32)
            score[y * zn + o] = s
            best = jnp.maximum(best, jnp.max(s.reshape(tj // 8, 8, count), axis=0))
        top[...] = best

    def up2(t): return ag_copy(4 * t, -2 * t, 2)
    def up1(t): return ag_copy(4 * t + 1, -2 * t, 1)
    def dn2(t): return ag_copy(4 * t + 2, 2 * t, -2)
    def dn1(t): return ag_copy(4 * t + 3, 2 * t, -1)

    sent = []

    def go(copy):
        copy.start()
        sent.append(copy)

    for t in range(hops):
        if t:
            up2(t - 1).wait_recv()
        go(up2(t))
        go(up1(t))
        if t:
            dn2(t - 1).wait_recv()
        if t < hops - 1:
            go(dn2(t))
        go(dn1(t))
        if t == 0:
            absorb(0)
        else:
            absorb(-2 * t)
            absorb(2 * t)
            up1(t - 1).wait_recv()
            absorb(-2 * t + 1)
            dn1(t - 1).wait_recv()
            absorb(2 * t - 1)
    up1(hops - 1).wait_recv()
    absorb(-2 * hops + 1)
    dn1(hops - 1).wait_recv()
    absorb(2 * hops - 1)
    up2(hops - 1).wait_recv()
    absorb(-2 * hops)

    largest = jnp.max(top[...], axis=0, keepdims=True)

    def first(b, carry):
        total, dots = carry
        p = jnp.exp(score[pl.ds(b * 2, 2)] - largest[None])
        score[pl.ds(b * 2, 2)] = p
        pd = p * dprob[pl.ds(b * 2, 2)]
        return (
            total + jnp.sum(p.reshape(2 * tj // 8, 8, count), axis=0),
            dots + jnp.sum(pd.reshape(2 * tj // 8, 8, count), axis=0),
        )

    zero = jnp.zeros((8, count), F32)
    total, dots = lax.fori_loop(0, samp // 2, first, (zero, zero))
    scale = 1.0 / jnp.sum(total, axis=0, keepdims=True)
    row_dot = jnp.sum(dots, axis=0, keepdims=True) * scale

    def second(b, carry):
        for y in range(YH):
            prob = score[y * zn + b] * scale
            probb[y, b] = prob.astype(BF16)
            dsb[y, b] = (prob * (dprob[y * zn + b] - row_dot)).astype(BF16)
        return carry

    lax.fori_loop(0, zn, second, 0)

    def rs_copy(sem, src, o):
        return pltpu.make_async_remote_copy(
            src_ref=src, dst_ref=rin.at[sem], send_sem=rs_send.at[sem], recv_sem=rs_recv.at[sem],
            device_id=at_z(o), device_id_type=MESH,
        )

    def own(o):
        return dsb.at[:, wrap(o)]

    def arrived(sem):
        rs_copy(sem, own(0), 1).wait_recv()
        return rin[sem].astype(F32)

    def one_matmul(k):
        p2 = probb[...].reshape(count, count) if k in (0, 3) else None
        d2 = dsb[...].reshape(count, count) if k in (1, 2) else None
        if k == 0:
            att_ref[...] = dot_nn(value, p2).astype(BF16)
        elif k == 1:
            qg_ref[...] = (dot_nn(key, d2) * inv_root).astype(BF16)
        elif k == 2:
            kg_ref[...] = (dot_nt(query, d2) * inv_root).astype(BF16)
        else:
            vg_ref[...] = dot_nt(grad, p2).astype(BF16)

    far = 2 * hops
    for t in range(hops):
        if t == 0:
            go(rs_copy(2, own(-far), -2))
        else:
            racc[2 * t] = (dsb[:, wrap(2 * t - far)].astype(F32) + arrived(4 * t - 2) + arrived(4 * t - 1)).astype(BF16)
            go(rs_copy(4 * t + 2, racc.at[2 * t], -2))
            acc = dsb[:, wrap(far - 2 * t)].astype(F32) + arrived(4 * t - 3)
            if t > 1:
                acc = acc + arrived(4 * t - 4)
            racc[2 * t + 1] = acc.astype(BF16)
            go(rs_copy(4 * t, racc.at[2 * t + 1], 2))
        go(rs_copy(4 * t + 3, own(2 * t + 1 - far), -1))
        go(rs_copy(4 * t + 1, own(far - 2 * t - 1), 1))
        for m in range(t * 4 // hops, (t + 1) * 4 // hops):
            one_matmul(m)
    last = 4 * hops
    acc = dsb[:, z].astype(F32) + arrived(last - 3) + arrived(last - 1) + arrived(last - 2)
    if hops > 1:
        acc = acc + arrived(last - 4)
    for t in range(tiles):
        fin[:, t] = acc[:, :, t * LANES : (t + 1) * LANES].astype(BF16)

    plane_send(lambda p: fin.at[p // heads, lax.rem(p, heads) // groups], brecv, b_send.at[0], b_recv.at[0])
    brecv[me_p] = fin[yh, me_h // groups]
    all_of(brecv, plane - 1, b_recv.at[0]).wait()
    tile32[...] = (brecv[0:heads].astype(F32) + brecv[heads:].astype(F32)).reshape(heads * tj, LANES)
    pieces = []
    for t in range(tj // groups):
        piece = jnp.zeros((heads, LANES), F32)
        for jj in range(groups):
            r = tile32[pl.ds(t * groups + jj, heads, stride=tj), :]
            turned = pltpu.roll(r, lax.rem(jj - grp + groups, groups) * ti, axis=1)
            piece = jnp.where(lane_group == jj, turned, piece)
        pieces.append(piece)
    bg = jnp.concatenate(pieces, axis=1)
    hi = bg.astype(BF16)
    lo = (bg - hi.astype(F32)).astype(BF16)
    wpart = dot_nn(hi, ln[...]) + dot_nn(lo, ln[...])
    lng = dot_tn(hi, wt) + dot_tn(lo, wt)
    for r in range(heads):
        part[r] = wpart[r : r + 1, :]
    part[heads] = jnp.sum(lng * norm[...], axis=0, keepdims=True)
    for r in range(heads + 1, plane):
        part[r] = jnp.zeros((1, LANES), F32)

    plane_send(lambda p: part.at[p], arr1, s1.at[0], r1.at[0])
    arr1[me_p] = part[me_p]

    for j in range(tj):
        rows = slice(j * ti, (j + 1) * ti)
        n = norm[rows, :]
        dn = lng[rows, :] * gain
        out = dn - jnp.mean(dn, axis=-1, keepdims=True) - n * jnp.mean(dn * n, axis=-1, keepdims=True)
        xs[pl.ds(j, ti, stride=tj), :] = out * inv[rows, :]
    pg_ref[...] = xs[...].reshape(ti, tj, LANES).astype(BF16)

    all_of(arr1, plane - 1, r1.at[0]).wait()
    row[...] = jnp.sum(arr1[...], axis=0)

    def z_send(off, c):
        pltpu.make_async_remote_copy(
            src_ref=row, dst_ref=arr2.at[z], send_sem=s2.at[0], recv_sem=r2.at[0],
            device_id=at_z(off), device_id_type=MESH,
        ).start()
        return c

    lax.fori_loop(1, zn, z_send, 0)
    arr2[z] = row[...]
    all_of(arr2, zn - 1, r2.at[0]).wait()
    tot[...] = jnp.sum(arr2[...], axis=0) * (1.0 / count)
    plane_send(lambda p: tot, res, s3.at[0], r3.at[0])
    res[me_p] = tot[...]
    all_of(res, plane - 1, r3.at[0]).wait()
    wg_ref[...] = jnp.concatenate([res[r] for r in range(heads)], axis=0)
    gg_ref[...] = res[heads]

    all_of(trecv, plane - 1, a_send.at[0]).wait()
    for copy in sent:
        copy.wait_send()
    all_of(brecv, plane - 1, b_send.at[0]).wait()
    all_of(arr1, plane - 1, s1.at[0]).wait()
    all_of(arr2, zn - 1, s2.at[0]).wait()
    all_of(res, plane - 1, s3.at[0]).wait()


def local(samp, heads, queries, keys, values, out_grad, pair, ln_gain, proj_weight, token_mask, atom_map):
    _, feat, count = queries.shape
    ti, tj, chan = pair.shape
    atoms = atom_map.shape[0]
    zn = samp // YH
    hops = zn // 4
    plane = YH * heads
    tiles = count // LANES
    vmem = pl.BlockSpec(memory_space=pltpu.VMEM)
    row = (1, LANES)
    dma = pltpu.SemaphoreType.DMA
    scratch = [
        pltpu.VMEM((max(ti * tj, count), LANES), F32),
        pltpu.VMEM((ti * tj, LANES), F32),
        pltpu.VMEM((ti * tj, LANES), F32),
        pltpu.VMEM((ti * tj, LANES), BF16),
        pltpu.VMEM((heads * tj, LANES), F32),
        pltpu.VMEM((heads, tj, LANES), BF16),
        pltpu.VMEM((plane, tj, LANES), BF16),
        pltpu.VMEM((YH, zn, tj, count), BF16),
        pltpu.VMEM((samp, tj, count), F32),
        pltpu.VMEM((samp, tj, count), F32),
        pltpu.VMEM((YH, zn, tj, count), BF16),
        pltpu.VMEM((YH, zn, tj, count), BF16),
        pltpu.VMEM((8, count), F32),
        pltpu.VMEM((4 * hops, YH, tj, count), BF16),
        pltpu.VMEM((2 * hops, YH, tj, count), BF16),
        pltpu.VMEM((YH, tiles, tj, LANES), BF16),
        pltpu.VMEM((plane, tj, LANES), BF16),
        pltpu.VMEM((plane,) + row, F32),
        pltpu.VMEM((plane,) + row, F32),
        pltpu.VMEM(row, F32),
        pltpu.VMEM((zn,) + row, F32),
        pltpu.VMEM(row, F32),
        pltpu.VMEM((plane,) + row, F32),
        dma((1,)), dma((1,)), dma((4 * hops,)), dma((4 * hops,)), dma((4 * hops,)), dma((4 * hops,)),
        dma((1,)), dma((1,)), dma((1,)), dma((1,)), dma((1,)), dma((1,)), dma((1,)), dma((1,)),
    ]
    shape = jax.ShapeDtypeStruct
    att, qg, kg, vg, pg, wg, gg = pl.pallas_call(
        functools.partial(kernel, samp, heads, atoms),
        out_shape=(
            shape((feat, count), BF16), shape((feat, count), BF16), shape((feat, count), BF16),
            shape((feat, count), BF16), shape((ti, tj, chan), BF16), shape((heads, chan), F32), shape((1, chan), F32),
        ),
        in_specs=[vmem] * 9,
        out_specs=(vmem,) * 7,
        scratch_shapes=scratch,
        compiler_params=pltpu.CompilerParams(
            collective_id=0, has_side_effects=True, vmem_limit_bytes=48 * 1024 * 1024
        ),
    )(
        queries[0], keys[0], values[0], out_grad[0], pair, ln_gain.reshape(1, chan), proj_weight.T,
        token_mask.reshape(tiles, LANES), atom_map.reshape(atoms // LANES, LANES),
    )
    return att[None], qg[None], kg[None], vg[None], pg, wg.T, gg[0]


def solution(mesh):
    cut = P("samp", "head", None)
    return jax.shard_map(
        functools.partial(local, mesh.shape["samp"], mesh.shape["head"]),
        mesh=mesh,
        in_specs=(cut, cut, cut, cut, P("head", "samp", None), P(), P(), P(), P()),
        out_specs=(cut, cut, cut, cut, P("head", "samp", None), P(), P()),
        check_vma=False,
    )
```

```python
import functools
import math

import jax
import jax.numpy as jnp
from jax import lax
from jax.experimental import pallas as pl
from jax.experimental.pallas import tpu as pltpu
from jax.sharding import PartitionSpec as P

MESH = pl.DeviceIdType.MESH
F32 = jnp.float32
BF16 = jnp.bfloat16
LANES = 128
YH = 2


def dot_nn(a, b):
    return lax.dot_general(a, b, (((1,), (0,)), ((), ())), preferred_element_type=F32)


def dot_nt(a, b):
    return lax.dot_general(a, b, (((1,), (1,)), ((), ())), preferred_element_type=F32)


def dot_tn(a, b):
    return lax.dot_general(a, b, (((0,), (0,)), ((), ())), preferred_element_type=F32)


def kernel(
    samp, heads, atoms,
    pair_hbm, gain_hbm, w_hbm, mask_hbm, atom_hbm, g_hbm, q_hbm, k_hbm, v_hbm,
    att_ref, qg_ref, kg_ref, vg_ref, pg_ref, wg_ref, gg_ref,
    pair_ref, gain_ref, w_ref, mask_ref, atom_ref, g_ref, q_ref, k_ref, v_ref,
    xs, norm, inv, ln, tile32, tsend, trecv, bias, score, dprob, probb, dsb, top,
    rin, racc, fin, brecv, part, arr1, row, arr2, tot, res,
    a_send, a_recv, ag_send, ag_recv, rs_send, rs_recv, b_send, b_recv,
    s1, r1, s2, r2, s3, r3, in_sem,
):
    arrays = (
        (pair_hbm, pair_ref), (gain_hbm, gain_ref), (w_hbm, w_ref), (mask_hbm, mask_ref), (atom_hbm, atom_ref),
        (g_hbm, g_ref), (q_hbm, q_ref), (k_hbm, k_ref), (v_hbm, v_ref),
    )
    loads = [pltpu.make_async_copy(src, dst, in_sem.at[i]) for i, (src, dst) in enumerate(arrays)]
    for load in loads:
        load.start()
    zn = samp // YH
    hops = zn // 4
    plane = YH * heads
    feat, count = q_ref.shape
    tj, ti = count // samp, count // heads
    groups = LANES // ti
    tiles = count // LANES
    inv_root = 1.0 / math.sqrt(feat)

    me_s, me_h = lax.axis_index("samp"), lax.axis_index("head")
    yh, z = me_s // zn, lax.rem(me_s, zn)
    me_p = yh * heads + me_h
    grp = lax.rem(me_h, groups)

    def at_plane(p):
        return (p // heads) * zn + z, lax.rem(p, heads)

    def wrap(o):
        return lax.rem(z + (o + 2 * zn), zn)

    def at_z(o):
        return yh * zn + wrap(o), me_h

    barrier = pltpu.get_barrier_semaphore()

    def greet(off, c):
        pl.semaphore_signal(barrier, inc=1, device_id=at_plane(lax.rem(me_p + off, plane)), device_id_type=MESH)
        return c

    lax.fori_loop(1, plane, greet, 0, unroll=True)
    for o in (1, -1, 2, -2):
        pl.semaphore_signal(barrier, inc=1, device_id=at_z(o), device_id_type=MESH)

    for load in loads[:3]:
        load.wait()

    gain = gain_ref[...]
    xs[...] = pair_ref[...].astype(F32).reshape(ti * tj, LANES)
    for j in range(tj):
        x = xs[pl.ds(j, ti, stride=tj), :]
        mu = jnp.mean(x, axis=-1, keepdims=True)
        d = x - mu
        iv = 1.0 / jnp.sqrt(jnp.mean(d * d, axis=-1, keepdims=True) + 1e-05)
        n = d * iv
        rows = slice(j * ti, (j + 1) * ti)
        norm[rows, :] = n
        inv[rows, :] = jnp.broadcast_to(iv, (ti, LANES))
        ln[rows, :] = (n * gain).astype(BF16)
    wt = w_ref[...]
    zb = dot_nt(wt, ln[...])
    lane_group = lax.broadcasted_iota(jnp.int32, (heads, LANES), 1) // ti
    for j in range(tj):
        t, jj = j // groups, j % groups
        turned = pltpu.roll(zb[:, t * LANES : (t + 1) * LANES], lax.rem(grp - jj + groups, groups) * ti, axis=1)
        tile32[pl.ds(j, heads, stride=tj), :] = jnp.where(lane_group == grp, turned, 0.0)
    tsend[...] = tile32[...].reshape(heads, tj, LANES).astype(BF16)

    pl.semaphore_wait(barrier, plane - 1 + 4)

    def all_of(ref, n, sem):
        return pltpu.make_async_copy(ref.at[pl.ds(0, n)], ref.at[pl.ds(0, n)], sem)

    def plane_send(src_of, dst, send, recv):
        def body(off, c):
            p = lax.rem(me_p + off, plane)
            pltpu.make_async_remote_copy(
                src_ref=src_of(p), dst_ref=dst.at[me_p], send_sem=send, recv_sem=recv,
                device_id=at_plane(p), device_id_type=MESH,
            ).start()
            return c

        lax.fori_loop(1, plane, body, 0, unroll=True)

    plane_send(lambda p: tsend.at[lax.rem(p, heads)], trecv, a_send.at[0], a_recv.at[0])
    trecv[me_p] = tsend[me_h]

    for load in loads[3:]:
        load.wait()
    length = jnp.sum(mask_ref[...].astype(F32), axis=(0, 1), keepdims=True)
    step = 64

    def counting(c, carry):
        ids = lax.broadcasted_iota(jnp.int32, (step, LANES), 0) + c * step
        acc = jnp.zeros((step, LANES), F32)
        for r in range(atoms // LANES):
            acc = acc + jnp.where(atom_ref[r : r + 1, :] == ids, 1.0, 0.0)
        xs[pl.ds(pl.multiple_of(c * step, step), step), :] = acc
        return carry

    lax.fori_loop(0, count // step, counting, 0)
    counts = dot_nt(jnp.ones((8, LANES), BF16), xs[0:count, :].astype(BF16))[0:1, :]
    real = lax.broadcasted_iota(jnp.int32, (1, count), 1).astype(F32) < length
    tok = jnp.where(real, counts * (count / atoms), 0.0)
    query, key, value = q_ref[...], k_ref[...], v_ref[...]
    grad = (g_ref[...].astype(F32) * tok).astype(BF16)
    chunk = LANES // tj
    top[...] = jnp.full(top.shape, -3.0e38, F32)

    def raw_scores():
        for c in range(tiles):
            cols = slice(c * LANES, (c + 1) * LANES)
            keep = lax.broadcasted_iota(jnp.int32, (LANES, 1), 0).astype(F32) + float(c * LANES) < length
            s = jnp.where(keep, dot_tn(key[:, cols], query) * inv_root, -1000000000.0)
            score[c * chunk : (c + 1) * chunk] = s.reshape(chunk, tj, count)

    def raw_dprob():
        for c in range(tiles):
            cols = slice(c * LANES, (c + 1) * LANES)
            dprob[c * chunk : (c + 1) * chunk] = dot_tn(value[:, cols], grad).reshape(chunk, tj, count)

    all_of(trecv, plane - 1, a_recv.at[0]).wait()
    for y in range(YH):
        for t in range(tiles):
            block = trecv[y * heads + t * groups]
            for u in range(1, groups):
                block = block + trecv[y * heads + t * groups + u]
            bias[y, z, :, t * LANES : (t + 1) * LANES] = block

    def ag_copy(sem, y, origin, o):
        return pltpu.make_async_remote_copy(
            src_ref=bias.at[y, wrap(origin)], dst_ref=bias.at[y, wrap(origin)],
            send_sem=ag_send.at[y, sem], recv_sem=ag_recv.at[y, sem], device_id=at_z(o), device_id_type=MESH,
        )

    def absorb(origin):
        o = wrap(origin)
        best = top[...]
        for y in range(YH):
            s = score[y * zn + o] + bias[y, o].astype(F32)
            score[y * zn + o] = s
            best = jnp.maximum(best, jnp.max(s.reshape(tj // 8, 8, count), axis=0))
        top[...] = best

    def up2(t, y): return ag_copy(4 * t, y, -2 * t, 2)
    def up1(t, y): return ag_copy(4 * t + 1, y, -2 * t, 1)
    def dn2(t, y): return ag_copy(4 * t + 2, y, 2 * t, -2)
    def dn1(t, y): return ag_copy(4 * t + 3, y, 2 * t, -1)

    sent = []

    def go(copy):
        copy.start()
        sent.append(copy)

    both = range(YH)
    for t in range(hops):
        for y in both:
            if t:
                up2(t - 1, y).wait_recv()
            go(up2(t, y))
            if t:
                dn2(t - 1, y).wait_recv()
            if t < hops - 1:
                go(dn2(t, y))
        for y in both:
            go(up1(t, y))
            go(dn1(t, y))
        if t == 0:
            raw_scores()
            absorb(0)
        else:
            if t == 1:
                raw_dprob()
            absorb(-2 * t)
            absorb(2 * t)
            for y in both:
                up1(t - 1, y).wait_recv()
                dn1(t - 1, y).wait_recv()
            absorb(-2 * t + 1)
            absorb(2 * t - 1)
    if hops == 1:
        raw_dprob()
    for y in both:
        up1(hops - 1, y).wait_recv()
        dn1(hops - 1, y).wait_recv()
    absorb(-2 * hops + 1)
    absorb(2 * hops - 1)
    for y in both:
        up2(hops - 1, y).wait_recv()
    absorb(-2 * hops)

    largest = jnp.max(top[...], axis=0, keepdims=True)

    def first(b, carry):
        total, dots = carry
        p = jnp.exp(score[pl.ds(b * 2, 2)] - largest[None])
        score[pl.ds(b * 2, 2)] = p
        pd = p * dprob[pl.ds(b * 2, 2)]
        return (
            total + jnp.sum(p.reshape(2 * tj // 8, 8, count), axis=0),
            dots + jnp.sum(pd.reshape(2 * tj // 8, 8, count), axis=0),
        )

    zero = jnp.zeros((8, count), F32)
    total, dots = lax.fori_loop(0, samp // 2, first, (zero, zero))
    scale = 1.0 / jnp.sum(total, axis=0, keepdims=True)
    row_dot = jnp.sum(dots, axis=0, keepdims=True) * scale

    def second(b, carry):
        for y in range(YH):
            prob = score[y * zn + b] * scale
            probb[y, b] = prob.astype(BF16)
            dsb[y, b] = (prob * (dprob[y * zn + b] - row_dot)).astype(BF16)
        return carry

    lax.fori_loop(0, zn, second, 0)

    def rs_copy(sem, y, src, o):
        return pltpu.make_async_remote_copy(
            src_ref=src, dst_ref=rin.at[sem, y], send_sem=rs_send.at[y, sem], recv_sem=rs_recv.at[y, sem],
            device_id=at_z(o), device_id_type=MESH,
        )

    def own(o, y):
        return dsb.at[y, wrap(o)]

    def mine(o, y):
        return dsb[y, wrap(o)].astype(F32)

    def arrived(sem, y):
        rs_copy(sem, y, own(0, y), 1).wait_recv()
        return rin[sem, y].astype(F32)

    def one_matmul(k):
        p2 = probb[...].reshape(count, count) if k in (0, 3) else None
        d2 = dsb[...].reshape(count, count) if k in (1, 2) else None
        if k == 0:
            att_ref[...] = dot_nn(value, p2).astype(BF16)
        elif k == 1:
            qg_ref[...] = (dot_nn(key, d2) * inv_root).astype(BF16)
        elif k == 2:
            kg_ref[...] = (dot_nt(query, d2) * inv_root).astype(BF16)
        else:
            vg_ref[...] = dot_nt(grad, p2).astype(BF16)

    far = 2 * hops

    def near(t):
        for y in both:
            go(rs_copy(4 * t + 3, y, own(2 * t + 1 - far, y), -1))
            go(rs_copy(4 * t + 1, y, own(far - 2 * t - 1, y), 1))

    for t in range(hops):
        for y in both:
            if t == 0:
                go(rs_copy(2, y, own(-far, y), -2))
            else:
                racc[2 * t, y] = (
                    mine(2 * t - far, y) + arrived(4 * t - 2, y) + arrived(4 * t - 1, y)
                ).astype(BF16)
                go(rs_copy(4 * t + 2, y, racc.at[2 * t, y], -2))
                acc = mine(far - 2 * t, y) + arrived(4 * t - 3, y)
                if t > 1:
                    acc = acc + arrived(4 * t - 4, y)
                racc[2 * t + 1, y] = acc.astype(BF16)
                go(rs_copy(4 * t, y, racc.at[2 * t + 1, y], 2))
        if t == 0:
            near(0)
        if t < hops - 1:
            near(t + 1)
        for m in range(t * 4 // hops, (t + 1) * 4 // hops):
            one_matmul(m)
    last = 4 * hops
    for y in both:
        acc = mine(0, y) + arrived(last - 3, y) + arrived(last - 1, y) + arrived(last - 2, y)
        if hops > 1:
            acc = acc + arrived(last - 4, y)
        for t in range(tiles):
            fin[y, t] = acc[:, t * LANES : (t + 1) * LANES].astype(BF16)

    plane_send(lambda p: fin.at[p // heads, lax.rem(p, heads) // groups], brecv, b_send.at[0], b_recv.at[0])
    brecv[me_p] = fin[yh, me_h // groups]
    all_of(brecv, plane - 1, b_recv.at[0]).wait()
    tile32[...] = (brecv[0:heads].astype(F32) + brecv[heads:].astype(F32)).reshape(heads * tj, LANES)
    pieces = []
    for t in range(tj // groups):
        piece = jnp.zeros((heads, LANES), F32)
        for jj in range(groups):
            r = tile32[pl.ds(t * groups + jj, heads, stride=tj), :]
            turned = pltpu.roll(r, lax.rem(jj - grp + groups, groups) * ti, axis=1)
            piece = jnp.where(lane_group == jj, turned, piece)
        pieces.append(piece)
    bg = jnp.concatenate(pieces, axis=1)
    hi = bg.astype(BF16)
    lo = (bg - hi.astype(F32)).astype(BF16)
    wpart = dot_nn(hi, ln[...]) + dot_nn(lo, ln[...])
    lng = dot_tn(hi, wt) + dot_tn(lo, wt)
    for r in range(heads):
        part[r] = wpart[r : r + 1, :]
    part[heads] = jnp.sum(lng * norm[...], axis=0, keepdims=True)
    for r in range(heads + 1, plane):
        part[r] = jnp.zeros((1, LANES), F32)

    plane_send(lambda p: part.at[p], arr1, s1.at[0], r1.at[0])
    arr1[me_p] = part[me_p]

    for j in range(tj):
        rows = slice(j * ti, (j + 1) * ti)
        n = norm[rows, :]
        dn = lng[rows, :] * gain
        out = dn - jnp.mean(dn, axis=-1, keepdims=True) - n * jnp.mean(dn * n, axis=-1, keepdims=True)
        xs[pl.ds(j, ti, stride=tj), :] = out * inv[rows, :]
    pg_ref[...] = xs[...].reshape(ti, tj, LANES).astype(BF16)

    all_of(arr1, plane - 1, r1.at[0]).wait()
    row[...] = jnp.sum(arr1[...], axis=0)

    def z_send(off, c):
        pltpu.make_async_remote_copy(
            src_ref=row, dst_ref=arr2.at[z], send_sem=s2.at[0], recv_sem=r2.at[0],
            device_id=at_z(off), device_id_type=MESH,
        ).start()
        return c

    lax.fori_loop(1, zn, z_send, 0, unroll=True)
    arr2[z] = row[...]
    all_of(arr2, zn - 1, r2.at[0]).wait()
    tot[...] = jnp.sum(arr2[...], axis=0) * (1.0 / count)
    plane_send(lambda p: tot, res, s3.at[0], r3.at[0])
    res[me_p] = tot[...]
    all_of(res, plane - 1, r3.at[0]).wait()
    wg_ref[...] = jnp.concatenate([res[r] for r in range(heads)], axis=0)
    gg_ref[...] = res[heads]

    all_of(trecv, plane - 1, a_send.at[0]).wait()
    for copy in sent:
        copy.wait_send()
    all_of(brecv, plane - 1, b_send.at[0]).wait()
    all_of(arr1, plane - 1, s1.at[0]).wait()
    all_of(arr2, zn - 1, s2.at[0]).wait()
    all_of(res, plane - 1, s3.at[0]).wait()


def put_out(*refs):
    sem = refs[-1]
    copies = [pltpu.make_async_copy(refs[i], refs[7 + i], sem.at[i]) for i in range(7)]
    for copy in copies:
        copy.start()
    for copy in copies:
        copy.wait()


def local(samp, heads, queries, keys, values, out_grad, pair, ln_gain, proj_weight, token_mask, atom_map):
    _, feat, count = queries.shape
    ti, tj, chan = pair.shape
    atoms = atom_map.shape[0]
    zn = samp // YH
    hops = zn // 4
    plane = YH * heads
    tiles = count // LANES
    vmem = pl.BlockSpec(memory_space=pltpu.VMEM)
    row = (1, LANES)
    dma = pltpu.SemaphoreType.DMA
    operands = (
        pair, ln_gain.reshape(1, chan), proj_weight.T, token_mask.reshape(tiles, LANES),
        atom_map.reshape(atoms // LANES, LANES), out_grad[0], queries[0], keys[0], values[0],
    )
    scratch = [pltpu.VMEM(x.shape, x.dtype) for x in operands] + [
        pltpu.VMEM((max(ti * tj, count), LANES), F32),
        pltpu.VMEM((ti * tj, LANES), F32),
        pltpu.VMEM((ti * tj, LANES), F32),
        pltpu.VMEM((ti * tj, LANES), BF16),
        pltpu.VMEM((heads * tj, LANES), F32),
        pltpu.VMEM((heads, tj, LANES), BF16),
        pltpu.VMEM((plane, tj, LANES), BF16),
        pltpu.VMEM((YH, zn, tj, count), BF16),
        pltpu.VMEM((samp, tj, count), F32),
        pltpu.VMEM((samp, tj, count), F32),
        pltpu.VMEM((YH, zn, tj, count), BF16),
        pltpu.VMEM((YH, zn, tj, count), BF16),
        pltpu.VMEM((8, count), F32),
        pltpu.VMEM((4 * hops, YH, tj, count), BF16),
        pltpu.VMEM((2 * hops, YH, tj, count), BF16),
        pltpu.VMEM((YH, tiles, tj, LANES), BF16),
        pltpu.VMEM((plane, tj, LANES), BF16),
        pltpu.VMEM((plane,) + row, F32),
        pltpu.VMEM((plane,) + row, F32),
        pltpu.VMEM(row, F32),
        pltpu.VMEM((zn,) + row, F32),
        pltpu.VMEM(row, F32),
        pltpu.VMEM((plane,) + row, F32),
        dma((1,)), dma((1,)), dma((YH, 4 * hops)), dma((YH, 4 * hops)), dma((YH, 4 * hops)), dma((YH, 4 * hops)),
        dma((1,)), dma((1,)), dma((1,)), dma((1,)), dma((1,)), dma((1,)), dma((1,)), dma((1,)), dma((9,)),
    ]
    shape = jax.ShapeDtypeStruct
    outs = (
        shape((feat, count), BF16), shape((feat, count), BF16), shape((feat, count), BF16),
        shape((feat, count), BF16), shape((ti, tj, chan), BF16), shape((heads, chan), F32), shape((1, chan), F32),
    )
    hbm = pl.BlockSpec(memory_space=pltpu.HBM)
    results = pl.pallas_call(
        functools.partial(kernel, samp, heads, atoms),
        out_shape=outs,
        in_specs=[hbm] * 9,
        out_specs=(vmem,) * 7,
        scratch_shapes=scratch,
        compiler_params=pltpu.CompilerParams(
            collective_id=0, has_side_effects=True, vmem_limit_bytes=48 * 1024 * 1024
        ),
    )(*(pltpu.with_memory_space_constraint(x, pltpu.HBM) for x in operands))
    att, qg, kg, vg, pg, wg, gg = pl.pallas_call(
        put_out,
        out_shape=outs,
        in_specs=[vmem] * 7,
        out_specs=(hbm,) * 7,
        scratch_shapes=[dma((7,))],
        compiler_params=pltpu.CompilerParams(vmem_limit_bytes=16 * 1024 * 1024),
    )(*results)
    return att[None], qg[None], kg[None], vg[None], pg, wg.T, gg[0]


def solution(mesh):
    cut = P("samp", "head", None)
    return jax.shard_map(
        functools.partial(local, mesh.shape["samp"], mesh.shape["head"]),
        mesh=mesh,
        in_specs=(cut, cut, cut, cut, P("head", "samp", None), P(), P(), P(), P()),
        out_specs=(cut, cut, cut, cut, P("head", "samp", None), P(), P()),
        check_vma=False,
    )
```

```python
import functools
import itertools
import math

import jax
import jax.numpy as jnp
from jax import lax
from jax.experimental import pallas as pl
from jax.experimental.pallas import tpu as pltpu
from jax.sharding import PartitionSpec as P

MESH = pl.DeviceIdType.MESH
F32 = jnp.float32
BF16 = jnp.bfloat16
LANES = 128
YH = 2


def dot_nn(a, b):
    return lax.dot_general(a, b, (((1,), (0,)), ((), ())), preferred_element_type=F32)


def dot_nt(a, b):
    return lax.dot_general(a, b, (((1,), (1,)), ((), ())), preferred_element_type=F32)


def dot_tn(a, b):
    return lax.dot_general(a, b, (((0,), (0,)), ((), ())), preferred_element_type=F32)


def kernel(
    samp, heads, atoms,
    pair_hbm, gain_hbm, w_hbm, mask_hbm, atom_hbm, g_hbm, q_hbm, k_hbm, v_hbm,
    att_ref, qg_ref, kg_ref, vg_ref, pg_ref, wg_ref, gg_ref,
    pair_ref, gain_ref, w_ref, mask_ref, atom_ref, g_ref, q_ref, k_ref, v_ref,
    ko_ref, vo_ref, qo_ref, go_ref, xs, norm, inv, ln, tile32, tsend, trecv, bias, score, dprob, probb, dsb, dsum, top,
    tx_half, rx_half, tx_whole, rx_whole,
    rin, racc, fin, brecv, part, arr1, row, arr2, tot, res,
    a_send, a_recv, ag_send, ag_recv, rs_send, rs_recv, b_send, b_recv,
    s1, r1, s2, r2, s3, r3, x_send, x_recv, y_send, y_recv, in_sem,
):
    arrays = (
        (pair_hbm, pair_ref), (gain_hbm, gain_ref), (w_hbm, w_ref), (mask_hbm, mask_ref), (atom_hbm, atom_ref),
        (k_hbm, k_ref), (v_hbm, v_ref),
    )
    feat, count = k_ref.shape
    half = count // YH
    for y in range(YH):
        arrays += ((q_hbm.at[:, y * half : (y + 1) * half], q_ref.at[y]), (g_hbm.at[:, y * half : (y + 1) * half], g_ref.at[y]))
    loads = [pltpu.make_async_copy(src, dst, in_sem.at[i]) for i, (src, dst) in enumerate(arrays)]
    for load in loads:
        load.start()
    zn = samp // YH
    plane = YH * heads
    tj, ti = count // samp, count // heads
    groups = LANES // ti
    tiles = count // LANES
    inv_root = 1.0 / math.sqrt(feat)

    me_s, me_h = lax.axis_index("samp"), lax.axis_index("head")
    yh, z = me_s // zn, lax.rem(me_s, zn)
    me_p = yh * heads + me_h
    share = heads // YH
    half_of_me = me_h // share
    mate = ((1 - yh) * zn + z, me_h)
    grp = lax.rem(me_h, groups)

    def at_plane(p):
        return (p // heads) * zn + z, lax.rem(p, heads)

    def wrap(o):
        return lax.rem(z + (o + 2 * zn), zn)

    def at_z(o):
        return yh * zn + wrap(o), me_h

    barrier = pltpu.get_barrier_semaphore()

    def greet(off, c):
        pl.semaphore_signal(barrier, inc=1, device_id=at_plane(lax.rem(me_p + off, plane)), device_id_type=MESH)
        return c

    lax.fori_loop(1, plane, greet, 0, unroll=True)
    near_far = (1, -1, 2, -2, zn // 4, -(zn // 4), zn // 2)
    for o in near_far:
        pl.semaphore_signal(barrier, inc=1, device_id=at_z(o), device_id_type=MESH)

    for load in loads[:3]:
        load.wait()

    gain = gain_ref[...]
    xs[...] = pair_ref[...].astype(F32).reshape(ti * tj, LANES)
    for j in range(tj):
        x = xs[pl.ds(j, ti, stride=tj), :]
        mu = jnp.mean(x, axis=-1, keepdims=True)
        d = x - mu
        iv = 1.0 / jnp.sqrt(jnp.mean(d * d, axis=-1, keepdims=True) + 1e-05)
        n = d * iv
        rows = slice(j * ti, (j + 1) * ti)
        norm[rows, :] = n
        inv[rows, :] = jnp.broadcast_to(iv, (ti, LANES))
        ln[rows, :] = (n * gain).astype(BF16)
    wt = w_ref[...]
    zb = dot_nt(wt, ln[...])
    lane_group = lax.broadcasted_iota(jnp.int32, (heads, LANES), 1) // ti
    for j in range(tj):
        t, jj = j // groups, j % groups
        turned = pltpu.roll(zb[:, t * LANES : (t + 1) * LANES], lax.rem(grp - jj + groups, groups) * ti, axis=1)
        tile32[pl.ds(j, heads, stride=tj), :] = jnp.where(lane_group == grp, turned, 0.0)
    tsend[...] = tile32[...].reshape(heads, tj, LANES).astype(BF16)

    pl.semaphore_wait(barrier, plane - 1 + len(near_far))

    def all_of(ref, n, sem):
        return pltpu.make_async_copy(ref.at[pl.ds(0, n)], ref.at[pl.ds(0, n)], sem)

    def plane_send(src_of, dst, send, recv):
        def body(off, c):
            p = lax.rem(me_p + off, plane)
            pltpu.make_async_remote_copy(
                src_ref=src_of(p), dst_ref=dst.at[me_p], send_sem=send, recv_sem=recv,
                device_id=at_plane(p), device_id_type=MESH,
            ).start()
            return c

        lax.fori_loop(1, plane, body, 0, unroll=True)

    slot = yh * share + lax.rem(me_h, share)

    def tile_out(h):
        return pltpu.make_async_remote_copy(
            src_ref=tsend.at[h], dst_ref=trecv.at[slot], send_sem=a_send.at[0], recv_sem=a_recv.at[0],
            device_id=(half_of_me * zn + z, h), device_id_type=MESH,
        )

    for b in range(1, heads):
        tile_out(lax.rem(me_h + b, heads)).start()

    @pl.when(half_of_me == yh)
    def _():
        pltpu.make_async_copy(tsend.at[me_h], trecv.at[slot], a_recv.at[0]).start()

    @pl.when(half_of_me != yh)
    def _():
        tile_out(me_h).start()

    for load in loads[3:]:
        load.wait()
    length = jnp.sum(mask_ref[...].astype(F32), axis=(0, 1), keepdims=True)
    step = 64

    def counting(c, carry):
        ids = lax.broadcasted_iota(jnp.int32, (step, LANES), 0) + (c * step + yh * half)
        acc = jnp.zeros((step, LANES), F32)
        for r in range(atoms // LANES):
            acc = acc + jnp.where(atom_ref[r : r + 1, :] == ids, 1.0, 0.0)
        xs[pl.ds(pl.multiple_of(c * step, step), step), :] = acc
        return carry

    lax.fori_loop(0, half // step, counting, 0)
    counts = dot_nt(jnp.ones((8, LANES), BF16), xs[0:half, :].astype(BF16))[0:1, :]
    real = (lax.broadcasted_iota(jnp.int32, (1, half), 1) + yh * half).astype(F32) < length
    tok = jnp.where(real, counts * (count / atoms), 0.0)
    chunk = LANES // tj
    top[...] = jnp.full(top.shape, -3.0e38, F32)

    def operands(sm):
        if sm:
            query, grad, key, value = qo_ref[...], go_ref[...], ko_ref[...], vo_ref[...]
        else:
            query, grad, key, value = q_ref[yh], g_ref[yh], k_ref[...], v_ref[...]
        return query, (grad.astype(F32) * tok).astype(BF16), key, value

    def raw(sm):
        query, grad, key, value = operands(sm)
        for c in range(tiles):
            cols = slice(c * LANES, (c + 1) * LANES)
            keep = lax.broadcasted_iota(jnp.int32, (LANES, 1), 0).astype(F32) + float(c * LANES) < length
            s = jnp.where(keep, dot_tn(key[:, cols], query) * inv_root, -1000000000.0)
            score[sm, c * chunk : (c + 1) * chunk] = s.reshape(chunk, tj, half)
            dprob[sm, c * chunk : (c + 1) * chunk] = dot_tn(value[:, cols], grad).reshape(chunk, tj, half)

    pltpu.make_async_copy(trecv, trecv, a_recv.at[0]).wait()
    for y in range(YH):
        for t in range(half // LANES):
            block = trecv[y * share + t * groups]
            for u in range(1, groups):
                block = block + trecv[y * share + t * groups + u]
            bias[y, z, :, t * LANES : (t + 1) * LANES] = block

    def ag_copy(sem, y, origin, o):
        return pltpu.make_async_remote_copy(
            src_ref=bias.at[y, wrap(origin)], dst_ref=bias.at[y, wrap(origin)],
            send_sem=ag_send.at[y, sem], recv_sem=ag_recv.at[y, sem], device_id=at_z(o), device_id_type=MESH,
        )

    def absorb(*origins):
        for y in range(YH):
            o = wrap(origins[(y + 1) % len(origins)])
            b = bias[y, o].astype(F32)
            for sm in range(YH):
                s = score[sm, y * zn + o] + b
                score[sm, y * zn + o] = s
                top[sm] = jnp.maximum(top[sm], jnp.max(s.reshape(tj // 8, 8, half), axis=0))

    both = range(YH)
    quarter = zn // 4
    member = (0, 2 * quarter, quarter, -quarter)

    def near(i, y):
        return (1, -1, 2 - 4 * y)[i]

    def far_copy(m, y):
        return ag_copy(m - 1, y, 0, -member[m])

    def near_copy(i, m, y):
        return ag_copy(3 + 4 * i + m, y, member[m], near(i, y))

    sent = []

    def go(copy):
        copy.start()
        sent.append(copy)

    def pass_on(m):
        for i in range(3):
            for y in both:
                go(near_copy(i, m, y))

    def take(m):
        for i in range(3):
            for y in both:
                near_copy(i, m, y).wait_recv()
        absorb(member[m] - 1)
        absorb(member[m] + 1)
        absorb(member[m] + 2, member[m] - 2)

    for m in (1, 2, 3):
        for y in both:
            go(far_copy(m, y))
    pass_on(0)

    def to_mate(src, dst, i, send, recv):
        return pltpu.make_async_remote_copy(
            src_ref=src, dst_ref=dst, send_sem=send.at[i], recv_sem=recv.at[i], device_id=mate, device_id_type=MESH,
        )

    swaps = [
        to_mate(src, dst, i, x_send, x_recv)
        for i, (src, dst) in enumerate(
            ((q_ref.at[1 - yh], qo_ref), (k_ref, ko_ref), (g_ref.at[1 - yh], go_ref), (v_ref, vo_ref))
        )
    ]
    for swap in swaps:
        go(swap)
    raw(0)
    for m in (2, 3):
        for y in both:
            far_copy(m, y).wait_recv()
        pass_on(m)
    for swap in swaps:
        swap.wait_recv()
    raw(1)
    absorb(0)
    absorb(member[2])
    absorb(member[3])
    take(0)
    for y in both:
        far_copy(1, y).wait_recv()
    pass_on(1)
    absorb(member[1])
    for m in (2, 3, 1):
        take(m)

    largest = [jnp.max(top[sm], axis=0, keepdims=True) for sm in both]

    def first(b, carry):
        new = []
        for sm in both:
            total, dots = carry[2 * sm], carry[2 * sm + 1]
            p = jnp.exp(score[sm, pl.ds(b * 2, 2)] - largest[sm][None])
            score[sm, pl.ds(b * 2, 2)] = p
            pd = p * dprob[sm, pl.ds(b * 2, 2)]
            new.append(total + jnp.sum(p.reshape(2 * tj // 8, 8, half), axis=0))
            new.append(dots + jnp.sum(pd.reshape(2 * tj // 8, 8, half), axis=0))
        return tuple(new)

    zero = jnp.zeros((8, half), F32)
    sums = lax.fori_loop(0, samp // 2, first, (zero,) * 4)
    scale = [1.0 / jnp.sum(sums[2 * sm], axis=0, keepdims=True) for sm in both]
    row_dot = [jnp.sum(sums[2 * sm + 1], axis=0, keepdims=True) * scale[sm] for sm in both]

    def second(b, carry):
        for y in both:
            both_ds = None
            for sm in both:
                prob = score[sm, y * zn + b] * scale[sm]
                probb[sm, y, b] = prob.astype(BF16)
                ds = prob * (dprob[sm, y * zn + b] - row_dot[sm])
                dsb[sm, y, b] = ds.astype(BF16)
                both_ds = ds if sm == 0 else both_ds + ds
            dsum[y, b] = both_ds.astype(BF16)
        return carry

    lax.fori_loop(0, zn, second, 0)

    def rs_copy(sem, y, src, o):
        return pltpu.make_async_remote_copy(
            src_ref=src, dst_ref=rin.at[sem, y], send_sem=rs_send.at[y, sem], recv_sem=rs_recv.at[y, sem],
            device_id=at_z(o), device_id_type=MESH,
        )

    def own(o, y):
        return dsum.at[y, wrap(o)]

    def mine(o, y):
        return dsum[y, wrap(o)].astype(F32)

    def arrived(sem, y):
        rs_copy(sem, y, own(0, y), 1).wait_recv()
        return rin[sem, y].astype(F32)

    def give(m):
        for i in range(3):
            for y in both:
                go(rs_copy(3 + 4 * i + m, y, own(near(i, y) + member[m], y), near(i, y)))

    def gather(m, y):
        return mine(member[m], y) + arrived(3 + m, y) + arrived(7 + m, y) + arrived(11 + m, y)

    def send_far(m):
        for y in both:
            racc[m - 1, y] = gather(m, y).astype(BF16)
            go(rs_copy(m - 1, y, racc.at[m - 1, y], member[m]))

    def rows_out(sm):
        query, grad, key, value = operands(sm)
        attended = dot_nn(value, probb[sm].reshape(count, half)).astype(BF16)
        query_grad = (dot_nn(key, dsb[sm].reshape(count, half)) * inv_root).astype(BF16)
        return attended, query_grad

    def columns_out(sm):
        query, grad, key, value = operands(sm)
        return dot_nt(query, dsb[sm].reshape(count, half)), dot_nt(grad, probb[sm].reshape(count, half))

    for m in (1, 2, 3):
        give(m)
    tx_half[0], tx_half[1] = rows_out(1)
    send_far(1)
    give(0)
    send_far(2)
    send_far(3)
    tx_whole[0], tx_whole[1] = columns_out(1)
    results = [
        to_mate(src, dst, i, y_send, y_recv)
        for i, (src, dst) in enumerate(((tx_half, rx_half), (tx_whole, rx_whole)))
    ]
    for result in results:
        go(result)
    att_ref[yh], qg_ref[yh] = rows_out(0)
    key_part, value_part = columns_out(0)
    for y in both:
        acc = gather(0, y) + arrived(1, y) + arrived(2, y) + arrived(0, y)
        for t in range(half // LANES):
            fin[y, t] = acc[:, t * LANES : (t + 1) * LANES].astype(BF16)

    def tile_back(dy, u):
        y = lax.rem(yh + dy, YH)
        place = lax.rem(me_h + u, share)
        return pltpu.make_async_remote_copy(
            src_ref=fin.at[y, place // groups], dst_ref=brecv.at[me_h], send_sem=b_send.at[0], recv_sem=b_recv.at[0],
            device_id=(y * zn + z, yh * share + place), device_id_type=MESH,
        )

    for dy, u in itertools.product(range(YH), range(share)):
        if dy or u:
            tile_back(dy, u).start()

    @pl.when(half_of_me == yh)
    def _():
        pltpu.make_async_copy(
            fin.at[yh, lax.rem(me_h, share) // groups], brecv.at[me_h], b_recv.at[0]
        ).start()

    @pl.when(half_of_me != yh)
    def _():
        tile_back(0, 0).start()

    pltpu.make_async_copy(brecv, brecv, b_recv.at[0]).wait()
    tile32[...] = brecv[...].astype(F32).reshape(heads * tj, LANES)
    pieces = []
    for t in range(tj // groups):
        piece = jnp.zeros((heads, LANES), F32)
        for jj in range(groups):
            r = tile32[pl.ds(t * groups + jj, heads, stride=tj), :]
            turned = pltpu.roll(r, lax.rem(jj - grp + groups, groups) * ti, axis=1)
            piece = jnp.where(lane_group == jj, turned, piece)
        pieces.append(piece)
    bg = jnp.concatenate(pieces, axis=1)
    hi = bg.astype(BF16)
    lo = (bg - hi.astype(F32)).astype(BF16)
    wpart = dot_nn(hi, ln[...]) + dot_nn(lo, ln[...])
    lng = dot_tn(hi, wt) + dot_tn(lo, wt)
    for r in range(heads):
        part[r] = wpart[r : r + 1, :]
    part[heads] = jnp.sum(lng * norm[...], axis=0, keepdims=True)
    for r in range(heads + 1, plane):
        part[r] = jnp.zeros((1, LANES), F32)

    plane_send(lambda p: part.at[p], arr1, s1.at[0], r1.at[0])
    arr1[me_p] = part[me_p]

    for j in range(tj):
        rows = slice(j * ti, (j + 1) * ti)
        n = norm[rows, :]
        dn = lng[rows, :] * gain
        out = dn - jnp.mean(dn, axis=-1, keepdims=True) - n * jnp.mean(dn * n, axis=-1, keepdims=True)
        xs[pl.ds(j, ti, stride=tj), :] = out * inv[rows, :]
    pg_ref[...] = xs[...].reshape(ti, tj, LANES).astype(BF16)

    for result in results:
        result.wait_recv()
    att_ref[1 - yh] = rx_half[0]
    qg_ref[1 - yh] = rx_half[1]
    kg_ref[...] = ((key_part + rx_whole[0]) * inv_root).astype(BF16)
    vg_ref[...] = (value_part + rx_whole[1]).astype(BF16)
    all_of(arr1, plane - 1, r1.at[0]).wait()
    row[...] = jnp.sum(arr1[...], axis=0)

    def z_send(off, c):
        pltpu.make_async_remote_copy(
            src_ref=row, dst_ref=arr2.at[z], send_sem=s2.at[0], recv_sem=r2.at[0],
            device_id=at_z(off), device_id_type=MESH,
        ).start()
        return c

    lax.fori_loop(1, zn, z_send, 0, unroll=True)
    arr2[z] = row[...]
    all_of(arr2, zn - 1, r2.at[0]).wait()
    tot[...] = jnp.sum(arr2[...], axis=0) * (1.0 / count)
    plane_send(lambda p: tot, res, s3.at[0], r3.at[0])
    res[me_p] = tot[...]
    all_of(res, plane - 1, r3.at[0]).wait()
    wg_ref[...] = jnp.concatenate([res[r] for r in range(heads)], axis=0)
    gg_ref[...] = res[heads]

    all_of(trecv, heads - 1, a_send.at[0]).wait()
    all_of(brecv, heads - 1, b_send.at[0]).wait()

    @pl.when(half_of_me != yh)
    def _():
        all_of(trecv, 1, a_send.at[0]).wait()
        all_of(brecv, 1, b_send.at[0]).wait()

    for copy in sent:
        copy.wait_send()
    all_of(arr1, plane - 1, s1.at[0]).wait()
    all_of(arr2, zn - 1, s2.at[0]).wait()
    all_of(res, plane - 1, s3.at[0]).wait()


def put_out(*refs):
    sem = refs[-1]
    half = refs[0].shape[2]
    pairs = [(refs[i].at[y], refs[7 + i].at[:, y * half : (y + 1) * half]) for i in range(2) for y in range(YH)]
    pairs += [(refs[i], refs[7 + i]) for i in range(2, 7)]
    copies = [pltpu.make_async_copy(src, dst, sem.at[i]) for i, (src, dst) in enumerate(pairs)]
    for copy in copies:
        copy.start()
    for copy in copies:
        copy.wait()


def local(samp, heads, queries, keys, values, out_grad, pair, ln_gain, proj_weight, token_mask, atom_map):
    _, feat, count = queries.shape
    ti, tj, chan = pair.shape
    atoms = atom_map.shape[0]
    zn = samp // YH
    plane = YH * heads
    tiles = count // LANES
    vmem = pl.BlockSpec(memory_space=pltpu.VMEM)
    row = (1, LANES)
    dma = pltpu.SemaphoreType.DMA
    operands = (
        pair, ln_gain.reshape(1, chan), proj_weight.T, token_mask.reshape(tiles, LANES),
        atom_map.reshape(atoms // LANES, LANES), out_grad[0], queries[0], keys[0], values[0],
    )
    half = count // YH
    halves = ((YH, feat, half), BF16)
    wide = ((feat, count), BF16)
    loaded = [(x.shape, x.dtype) for x in operands[:5]] + [halves, halves, wide, wide]
    loaded += [wide, wide, ((feat, half), BF16), ((feat, half), BF16)]
    scratch = [pltpu.VMEM(*x) for x in loaded] + [
        pltpu.VMEM((max(ti * tj, count), LANES), F32),
        pltpu.VMEM((ti * tj, LANES), F32),
        pltpu.VMEM((ti * tj, LANES), F32),
        pltpu.VMEM((ti * tj, LANES), BF16),
        pltpu.VMEM((heads * tj, LANES), F32),
        pltpu.VMEM((heads, tj, LANES), BF16),
        pltpu.VMEM((heads, tj, LANES), BF16),
        pltpu.VMEM((YH, zn, tj, half), BF16),
        pltpu.VMEM((YH, samp, tj, half), F32),
        pltpu.VMEM((YH, samp, tj, half), F32),
        pltpu.VMEM((YH, YH, zn, tj, half), BF16),
        pltpu.VMEM((YH, YH, zn, tj, half), BF16),
        pltpu.VMEM((YH, zn, tj, half), BF16),
        pltpu.VMEM((YH, 8, half), F32),
        pltpu.VMEM((2, feat, half), BF16),
        pltpu.VMEM((2, feat, half), BF16),
        pltpu.VMEM((2, feat, count), F32),
        pltpu.VMEM((2, feat, count), F32),
        pltpu.VMEM((15, YH, tj, half), BF16),
        pltpu.VMEM((3, YH, tj, half), BF16),
        pltpu.VMEM((YH, half // LANES, tj, LANES), BF16),
        pltpu.VMEM((heads, tj, LANES), BF16),
        pltpu.VMEM((plane,) + row, F32),
        pltpu.VMEM((plane,) + row, F32),
        pltpu.VMEM(row, F32),
        pltpu.VMEM((zn,) + row, F32),
        pltpu.VMEM(row, F32),
        pltpu.VMEM((plane,) + row, F32),
        dma((1,)), dma((1,)), dma((YH, 15)), dma((YH, 15)), dma((YH, 15)), dma((YH, 15)),
        dma((1,)), dma((1,)), dma((1,)), dma((1,)), dma((1,)), dma((1,)), dma((1,)), dma((1,)), dma((4,)), dma((4,)), dma((2,)), dma((2,)), dma((11,)),
    ]
    shape = jax.ShapeDtypeStruct
    tail = (
        shape((feat, count), BF16), shape((feat, count), BF16), shape((ti, tj, chan), BF16),
        shape((heads, chan), F32), shape((1, chan), F32),
    )
    outs = (shape((feat, count), BF16),) * 2 + tail
    hbm = pl.BlockSpec(memory_space=pltpu.HBM)
    results = pl.pallas_call(
        functools.partial(kernel, samp, heads, atoms),
        out_shape=(shape((YH, feat, half), BF16),) * 2 + tail,
        in_specs=[hbm] * 9,
        out_specs=(vmem,) * 7,
        scratch_shapes=scratch,
        compiler_params=pltpu.CompilerParams(
            collective_id=0, has_side_effects=True, vmem_limit_bytes=48 * 1024 * 1024
        ),
    )(*(pltpu.with_memory_space_constraint(x, pltpu.HBM) for x in operands))
    att, qg, kg, vg, pg, wg, gg = pl.pallas_call(
        put_out,
        out_shape=outs,
        in_specs=[vmem] * 7,
        out_specs=(hbm,) * 7,
        scratch_shapes=[dma((9,))],
        compiler_params=pltpu.CompilerParams(vmem_limit_bytes=16 * 1024 * 1024),
    )(*results)
    return att[None], qg[None], kg[None], vg[None], pg, wg.T, gg[0]


def solution(mesh):
    cut = P("samp", "head", None)
    return jax.shard_map(
        functools.partial(local, mesh.shape["samp"], mesh.shape["head"]),
        mesh=mesh,
        in_specs=(cut, cut, cut, cut, P("head", "samp", None), P(), P(), P(), P()),
        out_specs=(cut, cut, cut, cut, P("head", "samp", None), P(), P()),
        check_vma=False,
    )
```

```python
import functools
import itertools
import math

import jax
import jax.numpy as jnp
from jax import lax
from jax.experimental import pallas as pl
from jax.experimental.pallas import tpu as pltpu
from jax.sharding import PartitionSpec as P

MESH = pl.DeviceIdType.MESH
F32 = jnp.float32
BF16 = jnp.bfloat16
LANES = 128
YH = 2


def dot_nn(a, b):
    return lax.dot_general(a, b, (((1,), (0,)), ((), ())), preferred_element_type=F32)


def dot_nt(a, b):
    return lax.dot_general(a, b, (((1,), (1,)), ((), ())), preferred_element_type=F32)


def dot_tn(a, b):
    return lax.dot_general(a, b, (((0,), (0,)), ((), ())), preferred_element_type=F32)


def kernel(
    samp, heads, atoms,
    pair_hbm, gain_hbm, w_hbm, mask_hbm, atom_hbm, g_hbm, q_hbm, k_hbm, v_hbm,
    att_ref, qg_ref, kg_ref, vg_ref, pg_ref, wg_ref, gg_ref,
    pair_ref, gain_ref, w_ref, mask_ref, atom_ref, g_ref, q_ref, k_ref, v_ref,
    ko_ref, vo_ref, qo_ref, go_ref, xs, norm, inv, ln, tile32, tsend, trecv, bias, score, dprob, probb, dsb, dsum, top,
    tx_half, rx_half, tx_whole, rx_whole,
    rin, racc, fin, brecv, part, arr1, row, arr2, tot, res,
    a_send, a_recv, ag_send, ag_recv, rs_send, rs_recv, b_send, b_recv,
    s1, r1, s2, r2, s3, r3, x_send, x_recv, y_send, y_recv, in_sem, word,
):
    arrays = (
        (pair_hbm, pair_ref), (gain_hbm, gain_ref), (w_hbm, w_ref), (mask_hbm, mask_ref), (atom_hbm, atom_ref),
        (k_hbm, k_ref), (v_hbm, v_ref),
    )
    feat, count = k_ref.shape
    half = count // YH
    for y in range(YH):
        arrays += ((q_hbm.at[:, y * half : (y + 1) * half], q_ref.at[y]), (g_hbm.at[:, y * half : (y + 1) * half], g_ref.at[y]))
    loads = [pltpu.make_async_copy(src, dst, in_sem.at[i]) for i, (src, dst) in enumerate(arrays)]
    for load in loads:
        load.start()
    zn = samp // YH
    plane = YH * heads
    tj, ti = count // samp, count // heads
    groups = LANES // ti
    tiles = count // LANES
    inv_root = 1.0 / math.sqrt(feat)

    me_s, me_h = lax.axis_index("samp"), lax.axis_index("head")
    yh, z = me_s // zn, lax.rem(me_s, zn)
    me_p = yh * heads + me_h
    share = heads // YH
    half_of_me = me_h // share
    mate = ((1 - yh) * zn + z, me_h)
    grp = lax.rem(me_h, groups)

    along = heads // 4

    def turn(at, by, size):
        return jnp.where(at + by >= size, at + by - size, at + by)

    low, core = me_h // (heads // 2), lax.rem(me_h, 2)
    across = lax.rem(me_h // 2, along)
    row_of = [turn(low, d, 2) * (heads // 2) for d in range(2)]
    col_of = [turn(across, d, along) * 2 for d in range(along)]
    core_of = [turn(core, d, 2) for d in range(2)]
    high_of = [turn(yh, d, 2) for d in range(2)]
    samp_of = [h * zn + z for h in high_of]
    base_of = [h * heads for h in high_of]

    def steps(place):
        high, lo, x, c = place
        return (1 if lo else 2 * high) + min(x, along - x) + 0.1 * c

    places = sorted(itertools.product(range(2), range(2), range(along), range(2)), key=steps, reverse=True)[:-1]

    def head_at(lo, x, c):
        return row_of[lo] + col_of[x] + core_of[c]

    def at_place(place):
        high, lo, x, c = place
        return samp_of[high], head_at(lo, x, c)

    def wrap(o):
        by = o % zn
        return turn(z, by, zn) if by else z

    def at_z(o):
        return yh * zn + wrap(o), me_h

    barrier = pltpu.get_barrier_semaphore()

    for place in places:
        pl.semaphore_signal(barrier, inc=1, device_id=at_place(place), device_id_type=MESH)
    close = (1, -1, 2, -2)
    for o in close:
        pl.semaphore_signal(barrier, inc=1, device_id=at_z(o), device_id_type=MESH)

    for load in loads[:3]:
        load.wait()

    gain = gain_ref[...]
    xs[...] = pair_ref[...].astype(F32).reshape(ti * tj, LANES)
    for j in range(tj):
        x = xs[pl.ds(j, ti, stride=tj), :]
        mu = jnp.mean(x, axis=-1, keepdims=True)
        d = x - mu
        iv = 1.0 / jnp.sqrt(jnp.mean(d * d, axis=-1, keepdims=True) + 1e-05)
        n = d * iv
        rows = slice(j * ti, (j + 1) * ti)
        norm[rows, :] = n
        inv[rows, :] = jnp.broadcast_to(iv, (ti, LANES))
        ln[rows, :] = (n * gain).astype(BF16)
    wt = w_ref[...]
    zb = dot_nt(wt, ln[...])
    lane_group = lax.broadcasted_iota(jnp.int32, (heads, LANES), 1) // ti
    for j in range(tj):
        t, jj = j // groups, j % groups
        turned = pltpu.roll(zb[:, t * LANES : (t + 1) * LANES], lax.rem(grp - jj + groups, groups) * ti, axis=1)
        tile32[pl.ds(j, heads, stride=tj), :] = jnp.where(lane_group == grp, turned, 0.0)
    tsend[...] = tile32[...].reshape(heads, tj, LANES).astype(BF16)

    pl.semaphore_wait(barrier, plane - 1 + len(close))
    for o in (2, -2):
        pl.semaphore_signal(word.at[0], inc=1, device_id=at_z(o), device_id_type=MESH)

    def all_of(ref, n, sem):
        return pltpu.make_async_copy(ref.at[pl.ds(0, n)], ref.at[pl.ds(0, n)], sem)

    def plane_send(src_of, dst, send, recv):
        for place in places:
            samp_id, head_id = at_place(place)
            pltpu.make_async_remote_copy(
                src_ref=src_of(base_of[place[0]] + head_id), dst_ref=dst.at[me_p], send_sem=send, recv_sem=recv,
                device_id=(samp_id, head_id), device_id_type=MESH,
            ).start()

    slot = yh * share + lax.rem(me_h, share)

    def tile_out(h):
        return pltpu.make_async_remote_copy(
            src_ref=tsend.at[h], dst_ref=trecv.at[slot], send_sem=a_send.at[0], recv_sem=a_recv.at[0],
            device_id=(half_of_me * zn + z, h), device_id_type=MESH,
        )

    beside = [place[1:] for place in places if not place[0]]
    for place in beside:
        tile_out(head_at(*place)).start()

    @pl.when(half_of_me == yh)
    def _():
        pltpu.make_async_copy(tsend.at[me_h], trecv.at[slot], a_recv.at[0]).start()

    @pl.when(half_of_me != yh)
    def _():
        tile_out(me_h).start()

    pl.semaphore_wait(word.at[0], 2)
    for o in (4, -4):
        pl.semaphore_signal(word.at[1], inc=1, device_id=at_z(o), device_id_type=MESH)

    for load in loads[3:]:
        load.wait()
    length = jnp.sum(mask_ref[...].astype(F32), axis=(0, 1), keepdims=True)
    step = 64

    def counting(c, carry):
        ids = lax.broadcasted_iota(jnp.int32, (step, LANES), 0) + (c * step + yh * half)
        acc = jnp.zeros((step, LANES), F32)
        for r in range(atoms // LANES):
            acc = acc + jnp.where(atom_ref[r : r + 1, :] == ids, 1.0, 0.0)
        xs[pl.ds(pl.multiple_of(c * step, step), step), :] = acc
        return carry

    lax.fori_loop(0, half // step, counting, 0)
    counts = dot_nt(jnp.ones((8, LANES), BF16), xs[0:half, :].astype(BF16))[0:1, :]
    real = (lax.broadcasted_iota(jnp.int32, (1, half), 1) + yh * half).astype(F32) < length
    tok = jnp.where(real, counts * (count / atoms), 0.0)
    chunk = LANES // tj
    top[...] = jnp.full(top.shape, -3.0e38, F32)

    def operands(sm):
        if sm:
            query, grad, key, value = qo_ref[...], go_ref[...], ko_ref[...], vo_ref[...]
        else:
            query, grad, key, value = q_ref[yh], g_ref[yh], k_ref[...], v_ref[...]
        return query, (grad.astype(F32) * tok).astype(BF16), key, value

    def raw(sm):
        query, grad, key, value = operands(sm)
        for c in range(tiles):
            cols = slice(c * LANES, (c + 1) * LANES)
            keep = lax.broadcasted_iota(jnp.int32, (LANES, 1), 0).astype(F32) + float(c * LANES) < length
            s = jnp.where(keep, dot_tn(key[:, cols], query) * inv_root, -1000000000.0)
            score[sm, c * chunk : (c + 1) * chunk] = s.reshape(chunk, tj, half)
            dprob[sm, c * chunk : (c + 1) * chunk] = dot_tn(value[:, cols], grad).reshape(chunk, tj, half)

    pltpu.make_async_copy(trecv, trecv, a_recv.at[0]).wait()
    for y in range(YH):
        for t in range(half // LANES):
            block = trecv[y * share + t * groups]
            for u in range(1, groups):
                block = block + trecv[y * share + t * groups + u]
            bias[y, z, :, t * LANES : (t + 1) * LANES] = block

    def ag_copy(sem, y, origin, o):
        return pltpu.make_async_remote_copy(
            src_ref=bias.at[y, wrap(origin)], dst_ref=bias.at[y, wrap(origin)],
            send_sem=ag_send.at[y, sem], recv_sem=ag_recv.at[y, sem], device_id=at_z(o), device_id_type=MESH,
        )

    def absorb(*origins):
        for y in range(YH):
            o = wrap(origins[(y + 1) % len(origins)])
            b = bias[y, o].astype(F32)
            for sm in range(YH):
                s = score[sm, y * zn + o] + b
                score[sm, y * zn + o] = s
                top[sm] = jnp.maximum(top[sm], jnp.max(s.reshape(tj // 8, 8, half), axis=0))

    both = range(YH)
    quarter = zn // 4
    member = (0, 2 * quarter, quarter, -quarter)

    def near(i, y):
        return (1, -1, 2 - 4 * y)[i]

    def far_copy(m, y):
        return ag_copy(m - 1, y, 0, -member[m])

    def near_copy(i, m, y):
        return ag_copy(3 + 4 * i + m, y, member[m], near(i, y))

    sent = []

    def go(copy):
        copy.start()
        sent.append(copy)

    def pass_on(m):
        for i in range(3):
            for y in both:
                go(near_copy(i, m, y))

    def take(m):
        for i in range(3):
            for y in both:
                near_copy(i, m, y).wait_recv()
        absorb(member[m] - 1)
        absorb(member[m] + 1)
        absorb(member[m] + 2, member[m] - 2)

    pl.semaphore_wait(word.at[1], 2)
    def direct_copy(i, y):
        return ag_copy(4 + 4 * i, y, 0, member[1] + near(i, y))

    for m in (2, 3, 1):
        for y in both:
            go(far_copy(m, y))
    for i in range(3):
        for y in both:
            go(direct_copy(i, y))
    pass_on(0)

    def to_mate(src, dst, i, send, recv):
        return pltpu.make_async_remote_copy(
            src_ref=src, dst_ref=dst, send_sem=send.at[i], recv_sem=recv.at[i], device_id=mate, device_id_type=MESH,
        )

    swaps = [
        to_mate(src, dst, i, x_send, x_recv)
        for i, (src, dst) in enumerate(
            ((q_ref.at[1 - yh], qo_ref), (k_ref, ko_ref), (g_ref.at[1 - yh], go_ref), (v_ref, vo_ref))
        )
    ]
    for swap in swaps:
        go(swap)
    raw(0)
    for m in (2, 3):
        for y in both:
            far_copy(m, y).wait_recv()
        pass_on(m)
    for swap in swaps:
        swap.wait_recv()
    raw(1)
    absorb(0)
    absorb(member[2])
    absorb(member[3])
    take(0)
    for y in both:
        far_copy(1, y).wait_recv()
    absorb(member[1])
    for m in (2, 3, 1):
        take(m)

    largest = [jnp.max(top[sm], axis=0, keepdims=True) for sm in both]

    def first(b, carry):
        new = []
        for sm in both:
            total, dots = carry[2 * sm], carry[2 * sm + 1]
            p = jnp.exp(score[sm, pl.ds(b * 2, 2)] - largest[sm][None])
            score[sm, pl.ds(b * 2, 2)] = p
            pd = p * dprob[sm, pl.ds(b * 2, 2)]
            new.append(total + jnp.sum(p.reshape(2 * tj // 8, 8, half), axis=0))
            new.append(dots + jnp.sum(pd.reshape(2 * tj // 8, 8, half), axis=0))
        return tuple(new)

    zero = jnp.zeros((8, half), F32)
    sums = lax.fori_loop(0, samp // 2, first, (zero,) * 4)
    scale = [1.0 / jnp.sum(sums[2 * sm], axis=0, keepdims=True) for sm in both]
    row_dot = [jnp.sum(sums[2 * sm + 1], axis=0, keepdims=True) * scale[sm] for sm in both]

    def second(b, carry):
        for y in both:
            both_ds = None
            for sm in both:
                prob = score[sm, y * zn + b] * scale[sm]
                probb[sm, y, b] = prob.astype(BF16)
                ds = prob * (dprob[sm, y * zn + b] - row_dot[sm])
                dsb[sm, y, b] = ds.astype(BF16)
                both_ds = ds if sm == 0 else both_ds + ds
            dsum[y, b] = both_ds.astype(BF16)
        return carry

    lax.fori_loop(0, zn, second, 0)

    def rs_copy(sem, y, src, o):
        return pltpu.make_async_remote_copy(
            src_ref=src, dst_ref=rin.at[sem, y], send_sem=rs_send.at[y, sem], recv_sem=rs_recv.at[y, sem],
            device_id=at_z(o), device_id_type=MESH,
        )

    def own(o, y):
        return dsum.at[y, wrap(o)]

    def mine(o, y):
        return dsum[y, wrap(o)].astype(F32)

    def arrived(sem, y):
        rs_copy(sem, y, own(0, y), 1).wait_recv()
        return rin[sem, y].astype(F32)

    def give(m):
        for i in range(3):
            for y in both:
                o = near(i, y)
                go(rs_copy(3 + 4 * i + m, y, own(o + member[m], y), o + member[1] if m == 1 else o))

    def gather(m, y):
        return mine(member[m], y) + arrived(3 + m, y) + arrived(7 + m, y) + arrived(11 + m, y)

    def send_far(m):
        for y in both:
            if m == 1:
                go(rs_copy(0, y, own(member[1], y), member[1]))
            else:
                racc[m - 1, y] = gather(m, y).astype(BF16)
                go(rs_copy(m - 1, y, racc.at[m - 1, y], member[m]))

    def rows_out(sm):
        query, grad, key, value = operands(sm)
        attended = dot_nn(value, probb[sm].reshape(count, half)).astype(BF16)
        query_grad = (dot_nn(key, dsb[sm].reshape(count, half)) * inv_root).astype(BF16)
        return attended, query_grad

    def columns_out(sm):
        query, grad, key, value = operands(sm)
        return dot_nt(query, dsb[sm].reshape(count, half)), dot_nt(grad, probb[sm].reshape(count, half))

    give(2)
    give(3)
    send_far(1)
    give(1)
    give(0)
    tx_half[0], tx_half[1] = rows_out(1)
    send_far(2)
    send_far(3)
    tx_whole[0], tx_whole[1] = columns_out(1)
    results = [
        to_mate(src, dst, i, y_send, y_recv)
        for i, (src, dst) in enumerate(((tx_half, rx_half), (tx_whole, rx_whole)))
    ]
    for result in results:
        go(result)
    att_ref[yh], qg_ref[yh] = rows_out(0)
    key_part, value_part = columns_out(0)
    for y in both:
        acc = gather(0, y) + arrived(1, y) + arrived(2, y) + arrived(0, y) + arrived(4, y) + arrived(8, y) + arrived(12, y)
        for t in range(half // LANES):
            fin[y, t] = acc[:, t * LANES : (t + 1) * LANES].astype(BF16)

    def tile_back(high, x, c):
        spot = col_of[x] + core_of[c]
        return pltpu.make_async_remote_copy(
            src_ref=fin.at[high_of[high], spot // groups], dst_ref=brecv.at[me_h],
            send_sem=b_send.at[0], recv_sem=b_recv.at[0],
            device_id=(samp_of[high], yh * share + spot), device_id_type=MESH,
        )

    for high, lo, x, c in places:
        if not lo:
            tile_back(high, x, c).start()

    @pl.when(half_of_me == yh)
    def _():
        pltpu.make_async_copy(
            fin.at[yh, lax.rem(me_h, share) // groups], brecv.at[me_h], b_recv.at[0]
        ).start()

    @pl.when(half_of_me != yh)
    def _():
        tile_back(0, 0, 0).start()

    pltpu.make_async_copy(brecv, brecv, b_recv.at[0]).wait()
    tile32[...] = brecv[...].astype(F32).reshape(heads * tj, LANES)
    pieces = []
    for t in range(tj // groups):
        piece = jnp.zeros((heads, LANES), F32)
        for jj in range(groups):
            r = tile32[pl.ds(t * groups + jj, heads, stride=tj), :]
            turned = pltpu.roll(r, lax.rem(jj - grp + groups, groups) * ti, axis=1)
            piece = jnp.where(lane_group == jj, turned, piece)
        pieces.append(piece)
    bg = jnp.concatenate(pieces, axis=1)
    hi = bg.astype(BF16)
    lo = (bg - hi.astype(F32)).astype(BF16)
    wpart = dot_nn(hi, ln[...]) + dot_nn(lo, ln[...])
    lng = dot_tn(hi, wt) + dot_tn(lo, wt)
    for r in range(heads):
        part[r] = wpart[r : r + 1, :]
    part[heads] = jnp.sum(lng * norm[...], axis=0, keepdims=True)
    for r in range(heads + 1, plane):
        part[r] = jnp.zeros((1, LANES), F32)

    plane_send(lambda p: part.at[p], arr1, s1.at[0], r1.at[0])
    arr1[me_p] = part[me_p]

    for j in range(tj):
        rows = slice(j * ti, (j + 1) * ti)
        n = norm[rows, :]
        dn = lng[rows, :] * gain
        out = dn - jnp.mean(dn, axis=-1, keepdims=True) - n * jnp.mean(dn * n, axis=-1, keepdims=True)
        xs[pl.ds(j, ti, stride=tj), :] = out * inv[rows, :]
    pg_ref[...] = xs[...].reshape(ti, tj, LANES).astype(BF16)

    for result in results:
        result.wait_recv()
    att_ref[1 - yh] = rx_half[0]
    qg_ref[1 - yh] = rx_half[1]
    kg_ref[...] = ((key_part + rx_whole[0]) * inv_root).astype(BF16)
    vg_ref[...] = (value_part + rx_whole[1]).astype(BF16)
    all_of(arr1, plane - 1, r1.at[0]).wait()
    row[...] = jnp.sum(arr1[...], axis=0)

    for off in sorted(range(1, zn), key=lambda o: -min(o, zn - o)):
        pltpu.make_async_remote_copy(
            src_ref=row, dst_ref=arr2.at[z], send_sem=s2.at[0], recv_sem=r2.at[0],
            device_id=at_z(off), device_id_type=MESH,
        ).start()
    arr2[z] = row[...]
    all_of(arr2, zn - 1, r2.at[0]).wait()
    tot[...] = jnp.sum(arr2[...], axis=0) * (1.0 / count)
    plane_send(lambda p: tot, res, s3.at[0], r3.at[0])
    res[me_p] = tot[...]
    all_of(res, plane - 1, r3.at[0]).wait()
    wg_ref[...] = jnp.concatenate([res[r] for r in range(heads)], axis=0)
    gg_ref[...] = res[heads]

    all_of(trecv, heads - 1, a_send.at[0]).wait()
    all_of(brecv, heads - 1, b_send.at[0]).wait()

    @pl.when(half_of_me != yh)
    def _():
        all_of(trecv, 1, a_send.at[0]).wait()
        all_of(brecv, 1, b_send.at[0]).wait()

    for copy in sent:
        copy.wait_send()
    all_of(arr1, plane - 1, s1.at[0]).wait()
    all_of(arr2, zn - 1, s2.at[0]).wait()
    all_of(res, plane - 1, s3.at[0]).wait()


def put_out(*refs):
    sem = refs[-1]
    half = refs[0].shape[2]
    pairs = [(refs[i].at[y], refs[7 + i].at[:, y * half : (y + 1) * half]) for i in range(2) for y in range(YH)]
    pairs += [(refs[i], refs[7 + i]) for i in range(2, 7)]
    copies = [pltpu.make_async_copy(src, dst, sem.at[i]) for i, (src, dst) in enumerate(pairs)]
    for copy in copies:
        copy.start()
    for copy in copies:
        copy.wait()


def local(samp, heads, queries, keys, values, out_grad, pair, ln_gain, proj_weight, token_mask, atom_map):
    _, feat, count = queries.shape
    ti, tj, chan = pair.shape
    atoms = atom_map.shape[0]
    zn = samp // YH
    plane = YH * heads
    tiles = count // LANES
    vmem = pl.BlockSpec(memory_space=pltpu.VMEM)
    row = (1, LANES)
    dma = pltpu.SemaphoreType.DMA
    operands = (
        pair, ln_gain.reshape(1, chan), proj_weight.T, token_mask.reshape(tiles, LANES),
        atom_map.reshape(atoms // LANES, LANES), out_grad[0], queries[0], keys[0], values[0],
    )
    half = count // YH
    halves = ((YH, feat, half), BF16)
    wide = ((feat, count), BF16)
    loaded = [(x.shape, x.dtype) for x in operands[:5]] + [halves, halves, wide, wide]
    loaded += [wide, wide, ((feat, half), BF16), ((feat, half), BF16)]
    scratch = [pltpu.VMEM(*x) for x in loaded] + [
        pltpu.VMEM((max(ti * tj, count), LANES), F32),
        pltpu.VMEM((ti * tj, LANES), F32),
        pltpu.VMEM((ti * tj, LANES), F32),
        pltpu.VMEM((ti * tj, LANES), BF16),
        pltpu.VMEM((heads * tj, LANES), F32),
        pltpu.VMEM((heads, tj, LANES), BF16),
        pltpu.VMEM((heads, tj, LANES), BF16),
        pltpu.VMEM((YH, zn, tj, half), BF16),
        pltpu.VMEM((YH, samp, tj, half), F32),
        pltpu.VMEM((YH, samp, tj, half), F32),
        pltpu.VMEM((YH, YH, zn, tj, half), BF16),
        pltpu.VMEM((YH, YH, zn, tj, half), BF16),
        pltpu.VMEM((YH, zn, tj, half), BF16),
        pltpu.VMEM((YH, 8, half), F32),
        pltpu.VMEM((2, feat, half), BF16),
        pltpu.VMEM((2, feat, half), BF16),
        pltpu.VMEM((2, feat, count), F32),
        pltpu.VMEM((2, feat, count), F32),
        pltpu.VMEM((15, YH, tj, half), BF16),
        pltpu.VMEM((3, YH, tj, half), BF16),
        pltpu.VMEM((YH, half // LANES, tj, LANES), BF16),
        pltpu.VMEM((heads, tj, LANES), BF16),
        pltpu.VMEM((plane,) + row, F32),
        pltpu.VMEM((plane,) + row, F32),
        pltpu.VMEM(row, F32),
        pltpu.VMEM((zn,) + row, F32),
        pltpu.VMEM(row, F32),
        pltpu.VMEM((plane,) + row, F32),
        dma((1,)), dma((1,)), dma((YH, 15)), dma((YH, 15)), dma((YH, 15)), dma((YH, 15)),
        dma((1,)), dma((1,)), dma((1,)), dma((1,)), dma((1,)), dma((1,)), dma((1,)), dma((1,)), dma((4,)), dma((4,)), dma((2,)), dma((2,)), dma((11,)), pltpu.SemaphoreType.REGULAR((2,)),
    ]
    shape = jax.ShapeDtypeStruct
    tail = (
        shape((feat, count), BF16), shape((feat, count), BF16), shape((ti, tj, chan), BF16),
        shape((heads, chan), F32), shape((1, chan), F32),
    )
    outs = (shape((feat, count), BF16),) * 2 + tail
    hbm = pl.BlockSpec(memory_space=pltpu.HBM)
    results = pl.pallas_call(
        functools.partial(kernel, samp, heads, atoms),
        out_shape=(shape((YH, feat, half), BF16),) * 2 + tail,
        in_specs=[hbm] * 9,
        out_specs=(vmem,) * 7,
        scratch_shapes=scratch,
        compiler_params=pltpu.CompilerParams(
            collective_id=0, has_side_effects=True, vmem_limit_bytes=48 * 1024 * 1024
        ),
    )(*(pltpu.with_memory_space_constraint(x, pltpu.HBM) for x in operands))
    att, qg, kg, vg, pg, wg, gg = pl.pallas_call(
        put_out,
        out_shape=outs,
        in_specs=[vmem] * 7,
        out_specs=(hbm,) * 7,
        scratch_shapes=[dma((9,))],
        compiler_params=pltpu.CompilerParams(vmem_limit_bytes=16 * 1024 * 1024),
    )(*results)
    return att[None], qg[None], kg[None], vg[None], pg, wg.T, gg[0]


def solution(mesh):
    cut = P("samp", "head", None)
    return jax.shard_map(
        functools.partial(local, mesh.shape["samp"], mesh.shape["head"]),
        mesh=mesh,
        in_specs=(cut, cut, cut, cut, P("head", "samp", None), P(), P(), P(), P()),
        out_specs=(cut, cut, cut, cut, P("head", "samp", None), P(), P()),
        check_vma=False,
    )
```

```python
import functools
import itertools
import math

import jax
import jax.numpy as jnp
from jax import lax
from jax.experimental import pallas as pl
from jax.experimental.pallas import tpu as pltpu
from jax.sharding import PartitionSpec as P

MESH = pl.DeviceIdType.MESH
F32 = jnp.float32
BF16 = jnp.bfloat16
LANES = 128
YH = 2


def dot_nn(a, b):
    return lax.dot_general(a, b, (((1,), (0,)), ((), ())), preferred_element_type=F32)


def dot_nt(a, b):
    return lax.dot_general(a, b, (((1,), (1,)), ((), ())), preferred_element_type=F32)


def dot_tn(a, b):
    return lax.dot_general(a, b, (((0,), (0,)), ((), ())), preferred_element_type=F32)


def kernel(
    samp, heads, atoms,
    pair_hbm, gain_hbm, w_hbm, mask_hbm, atom_hbm, g_hbm, q_hbm, k_hbm, v_hbm,
    att_ref, qg_ref, kg_ref, vg_ref, pg_ref, wg_ref, gg_ref,
    pair_ref, gain_ref, w_ref, mask_ref, atom_ref, g_ref, q_ref, k_ref, v_ref,
    ko_ref, vo_ref, qo_ref, go_ref, xs, norm, inv, ln, tile32, tsend, trecv, bias, score, dprob, probb, dsb, dsum, top,
    tx_half, rx_half, tx_whole, rx_whole,
    rin, racc, fin, brecv, part, arr1, row, arr2, tot, res,
    a_send, a_recv, ag_send, ag_recv, rs_send, rs_recv, b_send, b_recv,
    s1, r1, s2, r2, s3, r3, x_send, x_recv, y_send, y_recv, in_sem, word,
):
    arrays = (
        (pair_hbm, pair_ref), (gain_hbm, gain_ref), (w_hbm, w_ref), (mask_hbm, mask_ref), (atom_hbm, atom_ref),
        (k_hbm, k_ref), (v_hbm, v_ref),
    )
    feat, count = k_ref.shape
    half = count // YH
    for y in range(YH):
        arrays += ((q_hbm.at[:, y * half : (y + 1) * half], q_ref.at[y]), (g_hbm.at[:, y * half : (y + 1) * half], g_ref.at[y]))
    loads = [pltpu.make_async_copy(src, dst, in_sem.at[i]) for i, (src, dst) in enumerate(arrays)]
    for load in loads:
        load.start()
    zn = samp // YH
    plane = YH * heads
    tj, ti = count // samp, count // heads
    groups = LANES // ti
    tiles = count // LANES
    inv_root = 1.0 / math.sqrt(feat)

    me_s, me_h = lax.axis_index("samp"), lax.axis_index("head")
    yh, z = me_s // zn, lax.rem(me_s, zn)
    me_p = yh * heads + me_h
    share = heads // YH
    half_of_me = me_h // share
    mate = ((1 - yh) * zn + z, me_h)
    grp = lax.rem(me_h, groups)

    along = heads // 4

    def turn(at, by, size):
        return jnp.where(at + by >= size, at + by - size, at + by)

    low, core = me_h // (heads // 2), lax.rem(me_h, 2)
    across = lax.rem(me_h // 2, along)
    row_of = [turn(low, d, 2) * (heads // 2) for d in range(2)]
    col_of = [turn(across, d, along) * 2 for d in range(along)]
    core_of = [turn(core, d, 2) for d in range(2)]
    high_of = [turn(yh, d, 2) for d in range(2)]
    samp_of = [h * zn + z for h in high_of]
    base_of = [h * heads for h in high_of]

    def steps(place):
        high, lo, x, c = place
        return (1 if lo else 2 * high) + min(x, along - x) + 0.1 * c

    places = sorted(itertools.product(range(2), range(2), range(along), range(2)), key=steps, reverse=True)[:-1]

    def head_at(lo, x, c):
        return row_of[lo] + col_of[x] + core_of[c]

    def at_place(place):
        high, lo, x, c = place
        return samp_of[high], head_at(lo, x, c)

    def wrap(o):
        by = o % zn
        return turn(z, by, zn) if by else z

    def at_z(o):
        return yh * zn + wrap(o), me_h

    barrier = pltpu.get_barrier_semaphore()

    for place in places:
        pl.semaphore_signal(barrier, inc=1, device_id=at_place(place), device_id_type=MESH)
    close = (1, -1, 2, -2)
    for o in close:
        pl.semaphore_signal(barrier, inc=1, device_id=at_z(o), device_id_type=MESH)

    for load in loads[:3]:
        load.wait()

    gain = gain_ref[...]
    xs[...] = pair_ref[...].astype(F32).reshape(ti * tj, LANES)
    for j in range(tj):
        x = xs[pl.ds(j, ti, stride=tj), :]
        mu = jnp.mean(x, axis=-1, keepdims=True)
        d = x - mu
        iv = 1.0 / jnp.sqrt(jnp.mean(d * d, axis=-1, keepdims=True) + 1e-05)
        n = d * iv
        rows = slice(j * ti, (j + 1) * ti)
        norm[rows, :] = n
        inv[rows, :] = jnp.broadcast_to(iv, (ti, LANES))
        ln[rows, :] = (n * gain).astype(BF16)
    wt = w_ref[...]
    zb = dot_nt(wt, ln[...])
    lane_group = lax.broadcasted_iota(jnp.int32, (heads, LANES), 1) // ti
    for j in range(tj):
        t, jj = j // groups, j % groups
        turned = pltpu.roll(zb[:, t * LANES : (t + 1) * LANES], lax.rem(grp - jj + groups, groups) * ti, axis=1)
        tile32[pl.ds(j, heads, stride=tj), :] = jnp.where(lane_group == grp, turned, 0.0)
    tsend[...] = tile32[...].reshape(heads, tj, LANES).astype(BF16)

    pl.semaphore_wait(barrier, plane - 1 + len(close))
    for o in (2, -2):
        pl.semaphore_signal(word.at[0], inc=1, device_id=at_z(o), device_id_type=MESH)

    def all_of(ref, n, sem):
        return pltpu.make_async_copy(ref.at[pl.ds(0, n)], ref.at[pl.ds(0, n)], sem)

    def plane_send(src_of, dst, send, recv):
        for place in places:
            samp_id, head_id = at_place(place)
            pltpu.make_async_remote_copy(
                src_ref=src_of(base_of[place[0]] + head_id), dst_ref=dst.at[me_p], send_sem=send, recv_sem=recv,
                device_id=(samp_id, head_id), device_id_type=MESH,
            ).start()

    slot = yh * share + lax.rem(me_h, share)

    def tile_out(h):
        return pltpu.make_async_remote_copy(
            src_ref=tsend.at[h], dst_ref=trecv.at[slot], send_sem=a_send.at[0], recv_sem=a_recv.at[0],
            device_id=(half_of_me * zn + z, h), device_id_type=MESH,
        )

    beside = [place[1:] for place in places if not place[0]]
    for place in beside:
        tile_out(head_at(*place)).start()

    @pl.when(half_of_me == yh)
    def _():
        pltpu.make_async_copy(tsend.at[me_h], trecv.at[slot], a_recv.at[0]).start()

    @pl.when(half_of_me != yh)
    def _():
        tile_out(me_h).start()

    pl.semaphore_wait(word.at[0], 2)
    for o in (4, -4):
        pl.semaphore_signal(word.at[1], inc=1, device_id=at_z(o), device_id_type=MESH)

    for load in loads[3:]:
        load.wait()
    length = jnp.sum(mask_ref[...].astype(F32), axis=(0, 1), keepdims=True)
    step = 64

    def counting(c, carry):
        ids = lax.broadcasted_iota(jnp.int32, (step, LANES), 0) + (c * step + yh * half)
        acc = jnp.zeros((step, LANES), F32)
        for r in range(atoms // LANES):
            acc = acc + jnp.where(atom_ref[r : r + 1, :] == ids, 1.0, 0.0)
        xs[pl.ds(pl.multiple_of(c * step, step), step), :] = acc
        return carry

    lax.fori_loop(0, half // step, counting, 0)
    counts = dot_nt(jnp.ones((8, LANES), BF16), xs[0:half, :].astype(BF16))[0:1, :]
    real = (lax.broadcasted_iota(jnp.int32, (1, half), 1) + yh * half).astype(F32) < length
    tok = jnp.where(real, counts * (count / atoms), 0.0)
    chunk = LANES // tj
    top[...] = jnp.full(top.shape, -3.0e38, F32)

    def operands(sm):
        if sm:
            query, grad, key, value = qo_ref[...], go_ref[...], ko_ref[...], vo_ref[...]
        else:
            query, grad, key, value = q_ref[yh], g_ref[yh], k_ref[...], v_ref[...]
        return query, (grad.astype(F32) * tok).astype(BF16), key, value

    def raw(sm):
        query, grad, key, value = operands(sm)
        for c in range(tiles):
            cols = slice(c * LANES, (c + 1) * LANES)
            keep = lax.broadcasted_iota(jnp.int32, (LANES, 1), 0).astype(F32) + float(c * LANES) < length
            s = jnp.where(keep, dot_tn(key[:, cols], query) * inv_root, -1000000000.0)
            score[sm, c * chunk : (c + 1) * chunk] = s.reshape(chunk, tj, half)
            dprob[sm, c * chunk : (c + 1) * chunk] = dot_tn(value[:, cols], grad).reshape(chunk, tj, half)

    pltpu.make_async_copy(trecv, trecv, a_recv.at[0]).wait()
    for y in range(YH):
        for t in range(half // LANES):
            block = trecv[y * share + t * groups]
            for u in range(1, groups):
                block = block + trecv[y * share + t * groups + u]
            bias[y, z, :, t * LANES : (t + 1) * LANES] = block

    def ag_copy(sem, y, origin, o):
        return pltpu.make_async_remote_copy(
            src_ref=bias.at[y, wrap(origin)], dst_ref=bias.at[y, wrap(origin)],
            send_sem=ag_send.at[y, sem], recv_sem=ag_recv.at[y, sem], device_id=at_z(o), device_id_type=MESH,
        )

    def absorb(*origins):
        for y in range(YH):
            o = wrap(origins[(y + 1) % len(origins)])
            b = bias[y, o].astype(F32)
            for sm in range(YH):
                s = score[sm, y * zn + o] + b
                score[sm, y * zn + o] = s
                top[sm] = jnp.maximum(top[sm], jnp.max(s.reshape(tj // 8, 8, half), axis=0))

    both = range(YH)

    def put(d, y, origin=0):
        return ag_copy(d + 7, y, origin, origin + d)

    sent = []

    def go(copy):
        copy.start()
        sent.append(copy)

    def pass_on(side):
        for d in (7, 6, 5, 3):
            for y in both:
                go(put(side * d, y, -4 * side))

    def take(*ds):
        for d in ds:
            for y in both:
                put(d, y).wait_recv()
            absorb(-d)

    pl.semaphore_wait(word.at[1], 2)
    for d in (4, -4, 8, 2, -2, 1, -1):
        for y in both:
            go(put(d, y))

    def to_mate(src, dst, i, send, recv):
        return pltpu.make_async_remote_copy(
            src_ref=src, dst_ref=dst, send_sem=send.at[i], recv_sem=recv.at[i], device_id=mate, device_id_type=MESH,
        )

    swaps = [
        to_mate(src, dst, i, x_send, x_recv)
        for i, (src, dst) in enumerate(
            ((q_ref.at[1 - yh], qo_ref), (k_ref, ko_ref), (g_ref.at[1 - yh], go_ref), (v_ref, vo_ref))
        )
    ]
    for swap in swaps:
        go(swap)
    raw(0)
    for side in (1, -1):
        for y in both:
            put(4 * side, y).wait_recv()
        pass_on(side)
    for swap in swaps:
        swap.wait_recv()
    raw(1)
    absorb(0)
    absorb(-4)
    absorb(4)
    take(1, -1, 2, -2, 3, -3, 8, 5, -5, 6, -6, 7, -7)

    largest = [jnp.max(top[sm], axis=0, keepdims=True) for sm in both]

    def first(b, carry):
        new = []
        for sm in both:
            total, dots = carry[2 * sm], carry[2 * sm + 1]
            p = jnp.exp(score[sm, pl.ds(b * 2, 2)] - largest[sm][None])
            score[sm, pl.ds(b * 2, 2)] = p
            pd = p * dprob[sm, pl.ds(b * 2, 2)]
            new.append(total + jnp.sum(p.reshape(2 * tj // 8, 8, half), axis=0))
            new.append(dots + jnp.sum(pd.reshape(2 * tj // 8, 8, half), axis=0))
        return tuple(new)

    zero = jnp.zeros((8, half), F32)
    sums = lax.fori_loop(0, samp // 2, first, (zero,) * 4)
    scale = [1.0 / jnp.sum(sums[2 * sm], axis=0, keepdims=True) for sm in both]
    row_dot = [jnp.sum(sums[2 * sm + 1], axis=0, keepdims=True) * scale[sm] for sm in both]

    def second(b, carry):
        for y in both:
            both_ds = None
            for sm in both:
                prob = score[sm, y * zn + b] * scale[sm]
                probb[sm, y, b] = prob.astype(BF16)
                ds = prob * (dprob[sm, y * zn + b] - row_dot[sm])
                dsb[sm, y, b] = ds.astype(BF16)
                both_ds = ds if sm == 0 else both_ds + ds
            dsum[y, b] = both_ds.astype(BF16)
        return carry

    lax.fori_loop(0, zn, second, 0)

    def rs_copy(sem, y, src, o):
        return pltpu.make_async_remote_copy(
            src_ref=src, dst_ref=rin.at[sem, y], send_sem=rs_send.at[y, sem], recv_sem=rs_recv.at[y, sem],
            device_id=at_z(o), device_id_type=MESH,
        )

    def own(o, y):
        return dsum.at[y, wrap(o)]

    def mine(o, y):
        return dsum[y, wrap(o)].astype(F32)

    def arrived(sem, y):
        rs_copy(sem, y, own(0, y), 1).wait_recv()
        return rin[sem, y].astype(F32)

    def give(d, hop):
        for y in both:
            go(rs_copy(d + 7, y, own(d, y), hop))

    def relay(side):
        for y in both:
            acc = mine(4 * side, y)
            for d in (3, 5, 6, 7):
                acc = acc + arrived(side * d + 7, y)
            racc[(side + 1) // 2, y] = acc.astype(BF16)
            go(rs_copy(4 * side + 7, y, racc.at[(side + 1) // 2, y], 4 * side))

    def rows_out(sm):
        query, grad, key, value = operands(sm)
        attended = dot_nn(value, probb[sm].reshape(count, half)).astype(BF16)
        query_grad = (dot_nn(key, dsb[sm].reshape(count, half)) * inv_root).astype(BF16)
        return attended, query_grad

    def columns_out(sm):
        query, grad, key, value = operands(sm)
        return dot_nt(query, dsb[sm].reshape(count, half)), dot_nt(grad, probb[sm].reshape(count, half))

    for d, hop in ((7, 3), (6, 2), (5, 1), (3, -1)):
        give(d, hop)
        give(-d, -hop)
    for d in (8, 2, -2, 1, -1):
        give(d, d)
    tx_half[0], tx_half[1] = rows_out(1)
    relay(1)
    relay(-1)
    tx_whole[0], tx_whole[1] = columns_out(1)
    results = [
        to_mate(src, dst, i, y_send, y_recv)
        for i, (src, dst) in enumerate(((tx_half, rx_half), (tx_whole, rx_whole)))
    ]
    for result in results:
        go(result)
    att_ref[yh], qg_ref[yh] = rows_out(0)
    key_part, value_part = columns_out(0)
    for y in both:
        acc = mine(0, y)
        for d in (1, -1, 2, -2, 8, 4, -4):
            acc = acc + arrived(d + 7, y)
        for t in range(half // LANES):
            fin[y, t] = acc[:, t * LANES : (t + 1) * LANES].astype(BF16)

    def tile_back(high, x, c):
        spot = col_of[x] + core_of[c]
        return pltpu.make_async_remote_copy(
            src_ref=fin.at[high_of[high], spot // groups], dst_ref=brecv.at[me_h],
            send_sem=b_send.at[0], recv_sem=b_recv.at[0],
            device_id=(samp_of[high], yh * share + spot), device_id_type=MESH,
        )

    for high, lo, x, c in places:
        if not lo:
            tile_back(high, x, c).start()

    @pl.when(half_of_me == yh)
    def _():
        pltpu.make_async_copy(
            fin.at[yh, lax.rem(me_h, share) // groups], brecv.at[me_h], b_recv.at[0]
        ).start()

    @pl.when(half_of_me != yh)
    def _():
        tile_back(0, 0, 0).start()

    pltpu.make_async_copy(brecv, brecv, b_recv.at[0]).wait()
    tile32[...] = brecv[...].astype(F32).reshape(heads * tj, LANES)
    pieces = []
    for t in range(tj // groups):
        piece = jnp.zeros((heads, LANES), F32)
        for jj in range(groups):
            r = tile32[pl.ds(t * groups + jj, heads, stride=tj), :]
            turned = pltpu.roll(r, lax.rem(jj - grp + groups, groups) * ti, axis=1)
            piece = jnp.where(lane_group == jj, turned, piece)
        pieces.append(piece)
    bg = jnp.concatenate(pieces, axis=1)
    hi = bg.astype(BF16)
    lo = (bg - hi.astype(F32)).astype(BF16)
    wpart = dot_nn(hi, ln[...]) + dot_nn(lo, ln[...])
    lng = dot_tn(hi, wt) + dot_tn(lo, wt)
    for r in range(heads):
        part[r] = wpart[r : r + 1, :]
    part[heads] = jnp.sum(lng * norm[...], axis=0, keepdims=True)
    for r in range(heads + 1, plane):
        part[r] = jnp.zeros((1, LANES), F32)

    plane_send(lambda p: part.at[p], arr1, s1.at[0], r1.at[0])
    arr1[me_p] = part[me_p]

    for j in range(tj):
        rows = slice(j * ti, (j + 1) * ti)
        n = norm[rows, :]
        dn = lng[rows, :] * gain
        out = dn - jnp.mean(dn, axis=-1, keepdims=True) - n * jnp.mean(dn * n, axis=-1, keepdims=True)
        xs[pl.ds(j, ti, stride=tj), :] = out * inv[rows, :]
    pg_ref[...] = xs[...].reshape(ti, tj, LANES).astype(BF16)

    for result in results:
        result.wait_recv()
    att_ref[1 - yh] = rx_half[0]
    qg_ref[1 - yh] = rx_half[1]
    kg_ref[...] = ((key_part + rx_whole[0]) * inv_root).astype(BF16)
    vg_ref[...] = (value_part + rx_whole[1]).astype(BF16)
    all_of(arr1, plane - 1, r1.at[0]).wait()
    row[...] = jnp.sum(arr1[...], axis=0)

    for off in sorted(range(1, zn), key=lambda o: -min(o, zn - o)):
        pltpu.make_async_remote_copy(
            src_ref=row, dst_ref=arr2.at[z], send_sem=s2.at[0], recv_sem=r2.at[0],
            device_id=at_z(off), device_id_type=MESH,
        ).start()
    arr2[z] = row[...]
    all_of(arr2, zn - 1, r2.at[0]).wait()
    tot[...] = jnp.sum(arr2[...], axis=0) * (1.0 / count)
    plane_send(lambda p: tot, res, s3.at[0], r3.at[0])
    res[me_p] = tot[...]
    all_of(res, plane - 1, r3.at[0]).wait()
    wg_ref[...] = jnp.concatenate([res[r] for r in range(heads)], axis=0)
    gg_ref[...] = res[heads]

    all_of(trecv, heads - 1, a_send.at[0]).wait()
    all_of(brecv, heads - 1, b_send.at[0]).wait()

    @pl.when(half_of_me != yh)
    def _():
        all_of(trecv, 1, a_send.at[0]).wait()
        all_of(brecv, 1, b_send.at[0]).wait()

    for copy in sent:
        copy.wait_send()
    all_of(arr1, plane - 1, s1.at[0]).wait()
    all_of(arr2, zn - 1, s2.at[0]).wait()
    all_of(res, plane - 1, s3.at[0]).wait()


def put_out(*refs):
    sem = refs[-1]
    half = refs[0].shape[2]
    pairs = [(refs[i].at[y], refs[7 + i].at[:, y * half : (y + 1) * half]) for i in range(2) for y in range(YH)]
    pairs += [(refs[i], refs[7 + i]) for i in range(2, 7)]
    copies = [pltpu.make_async_copy(src, dst, sem.at[i]) for i, (src, dst) in enumerate(pairs)]
    for copy in copies:
        copy.start()
    for copy in copies:
        copy.wait()


def local(samp, heads, queries, keys, values, out_grad, pair, ln_gain, proj_weight, token_mask, atom_map):
    _, feat, count = queries.shape
    ti, tj, chan = pair.shape
    atoms = atom_map.shape[0]
    zn = samp // YH
    plane = YH * heads
    tiles = count // LANES
    vmem = pl.BlockSpec(memory_space=pltpu.VMEM)
    row = (1, LANES)
    dma = pltpu.SemaphoreType.DMA
    operands = (
        pair, ln_gain.reshape(1, chan), proj_weight.T, token_mask.reshape(tiles, LANES),
        atom_map.reshape(atoms // LANES, LANES), out_grad[0], queries[0], keys[0], values[0],
    )
    half = count // YH
    halves = ((YH, feat, half), BF16)
    wide = ((feat, count), BF16)
    loaded = [(x.shape, x.dtype) for x in operands[:5]] + [halves, halves, wide, wide]
    loaded += [wide, wide, ((feat, half), BF16), ((feat, half), BF16)]
    scratch = [pltpu.VMEM(*x) for x in loaded] + [
        pltpu.VMEM((max(ti * tj, count), LANES), F32),
        pltpu.VMEM((ti * tj, LANES), F32),
        pltpu.VMEM((ti * tj, LANES), F32),
        pltpu.VMEM((ti * tj, LANES), BF16),
        pltpu.VMEM((heads * tj, LANES), F32),
        pltpu.VMEM((heads, tj, LANES), BF16),
        pltpu.VMEM((heads, tj, LANES), BF16),
        pltpu.VMEM((YH, zn, tj, half), BF16),
        pltpu.VMEM((YH, samp, tj, half), F32),
        pltpu.VMEM((YH, samp, tj, half), F32),
        pltpu.VMEM((YH, YH, zn, tj, half), BF16),
        pltpu.VMEM((YH, YH, zn, tj, half), BF16),
        pltpu.VMEM((YH, zn, tj, half), BF16),
        pltpu.VMEM((YH, 8, half), F32),
        pltpu.VMEM((2, feat, half), BF16),
        pltpu.VMEM((2, feat, half), BF16),
        pltpu.VMEM((2, feat, count), F32),
        pltpu.VMEM((2, feat, count), F32),
        pltpu.VMEM((16, YH, tj, half), BF16),
        pltpu.VMEM((2, YH, tj, half), BF16),
        pltpu.VMEM((YH, half // LANES, tj, LANES), BF16),
        pltpu.VMEM((heads, tj, LANES), BF16),
        pltpu.VMEM((plane,) + row, F32),
        pltpu.VMEM((plane,) + row, F32),
        pltpu.VMEM(row, F32),
        pltpu.VMEM((zn,) + row, F32),
        pltpu.VMEM(row, F32),
        pltpu.VMEM((plane,) + row, F32),
        dma((1,)), dma((1,)), dma((YH, 16)), dma((YH, 16)), dma((YH, 16)), dma((YH, 16)),
        dma((1,)), dma((1,)), dma((1,)), dma((1,)), dma((1,)), dma((1,)), dma((1,)), dma((1,)), dma((4,)), dma((4,)), dma((2,)), dma((2,)), dma((11,)), pltpu.SemaphoreType.REGULAR((2,)),
    ]
    shape = jax.ShapeDtypeStruct
    tail = (
        shape((feat, count), BF16), shape((feat, count), BF16), shape((ti, tj, chan), BF16),
        shape((heads, chan), F32), shape((1, chan), F32),
    )
    outs = (shape((feat, count), BF16),) * 2 + tail
    hbm = pl.BlockSpec(memory_space=pltpu.HBM)
    results = pl.pallas_call(
        functools.partial(kernel, samp, heads, atoms),
        out_shape=(shape((YH, feat, half), BF16),) * 2 + tail,
        in_specs=[hbm] * 9,
        out_specs=(vmem,) * 7,
        scratch_shapes=scratch,
        compiler_params=pltpu.CompilerParams(
            collective_id=0, has_side_effects=True, vmem_limit_bytes=48 * 1024 * 1024
        ),
    )(*(pltpu.with_memory_space_constraint(x, pltpu.HBM) for x in operands))
    att, qg, kg, vg, pg, wg, gg = pl.pallas_call(
        put_out,
        out_shape=outs,
        in_specs=[vmem] * 7,
        out_specs=(hbm,) * 7,
        scratch_shapes=[dma((9,))],
        compiler_params=pltpu.CompilerParams(vmem_limit_bytes=16 * 1024 * 1024),
    )(*results)
    return att[None], qg[None], kg[None], vg[None], pg, wg.T, gg[0]


def solution(mesh):
    cut = P("samp", "head", None)
    return jax.shard_map(
        functools.partial(local, mesh.shape["samp"], mesh.shape["head"]),
        mesh=mesh,
        in_specs=(cut, cut, cut, cut, P("head", "samp", None), P(), P(), P(), P()),
        out_specs=(cut, cut, cut, cut, P("head", "samp", None), P(), P()),
        check_vma=False,
    )
```

```python
import functools
import itertools
import math

import jax
import jax.numpy as jnp
from jax import lax
from jax.experimental import pallas as pl
from jax.experimental.pallas import tpu as pltpu
from jax.sharding import PartitionSpec as P

MESH = pl.DeviceIdType.MESH
F32 = jnp.float32
BF16 = jnp.bfloat16
LANES = 128
YH = 2


def dot_nn(a, b):
    return lax.dot_general(a, b, (((1,), (0,)), ((), ())), preferred_element_type=F32)


def dot_nt(a, b):
    return lax.dot_general(a, b, (((1,), (1,)), ((), ())), preferred_element_type=F32)


def dot_tn(a, b):
    return lax.dot_general(a, b, (((0,), (0,)), ((), ())), preferred_element_type=F32)


def kernel(
    samp, heads, atoms,
    pair_hbm, gain_hbm, w_hbm, mask_hbm, atom_hbm, g_hbm, q_hbm, k_hbm, v_hbm,
    att_ref, qg_ref, kg_ref, vg_ref, pg_ref, wg_ref, gg_ref,
    pair_ref, gain_ref, w_ref, mask_ref, atom_ref, g_ref, q_ref, k_ref, v_ref,
    ko_ref, vo_ref, qo_ref, go_ref, xs, norm, inv, ln, tile32, tsend, trecv, bias, score, dprob, probb, dsb, dsum, top,
    tx_half, rx_half, tx_whole, rx_whole,
    rin, racc, fin, brecv, part, arr1, row, arr2, tot, res,
    a_send, a_recv, ag_send, ag_recv, rs_send, rs_recv, b_send, b_recv,
    s1, r1, s2, r2, s3, r3, x_send, x_recv, y_send, y_recv, in_sem, word,
):
    arrays = (
        (pair_hbm, pair_ref), (gain_hbm, gain_ref), (w_hbm, w_ref), (mask_hbm, mask_ref), (atom_hbm, atom_ref),
        (k_hbm, k_ref), (v_hbm, v_ref),
    )
    feat, count = k_ref.shape
    half = count // YH
    for y in range(YH):
        arrays += ((q_hbm.at[:, y * half : (y + 1) * half], q_ref.at[y]), (g_hbm.at[:, y * half : (y + 1) * half], g_ref.at[y]))
    loads = [pltpu.make_async_copy(src, dst, in_sem.at[i]) for i, (src, dst) in enumerate(arrays)]
    for load in loads:
        load.start()
    zn = samp // YH
    plane = YH * heads
    tj, ti = count // samp, count // heads
    groups = LANES // ti
    tiles = count // LANES
    inv_root = 1.0 / math.sqrt(feat)

    me_s, me_h = lax.axis_index("samp"), lax.axis_index("head")
    yh, z = me_s // zn, lax.rem(me_s, zn)
    me_p = yh * heads + me_h
    share = heads // YH
    half_of_me = me_h // share
    mate = ((1 - yh) * zn + z, me_h)
    grp = lax.rem(me_h, groups)

    along = heads // 4

    def turn(at, by, size):
        return jnp.where(at + by >= size, at + by - size, at + by)

    low, core = me_h // (heads // 2), lax.rem(me_h, 2)
    across = lax.rem(me_h // 2, along)
    row_of = [turn(low, d, 2) * (heads // 2) for d in range(2)]
    col_of = [turn(across, d, along) * 2 for d in range(along)]
    core_of = [turn(core, d, 2) for d in range(2)]
    high_of = [turn(yh, d, 2) for d in range(2)]
    samp_of = [h * zn + z for h in high_of]
    base_of = [h * heads for h in high_of]

    def steps(place):
        high, lo, x, c = place
        return (1 if lo else 2 * high) + min(x, along - x) + 0.1 * c

    places = sorted(itertools.product(range(2), range(2), range(along), range(2)), key=steps, reverse=True)[:-1]

    def head_at(lo, x, c):
        return row_of[lo] + col_of[x] + core_of[c]

    def at_place(place):
        high, lo, x, c = place
        return samp_of[high], head_at(lo, x, c)

    def wrap(o):
        by = o % zn
        return turn(z, by, zn) if by else z

    def at_z(o):
        return yh * zn + wrap(o), me_h

    barrier = pltpu.get_barrier_semaphore()

    for place in places:
        pl.semaphore_signal(barrier, inc=1, device_id=at_place(place), device_id_type=MESH)
    close = (1, -1, 2, -2)
    for o in close:
        pl.semaphore_signal(barrier, inc=1, device_id=at_z(o), device_id_type=MESH)

    for load in loads[:3]:
        load.wait()

    gain = gain_ref[...]
    xs[...] = pair_ref[...].astype(F32).reshape(ti * tj, LANES)
    for j in range(tj):
        x = xs[pl.ds(j, ti, stride=tj), :]
        mu = jnp.mean(x, axis=-1, keepdims=True)
        d = x - mu
        iv = 1.0 / jnp.sqrt(jnp.mean(d * d, axis=-1, keepdims=True) + 1e-05)
        n = d * iv
        rows = slice(j * ti, (j + 1) * ti)
        norm[rows, :] = n
        inv[rows, :] = jnp.broadcast_to(iv, (ti, LANES))
        ln[rows, :] = (n * gain).astype(BF16)
    wt = w_ref[...]
    zb = dot_nt(wt, ln[...])
    lane_group = lax.broadcasted_iota(jnp.int32, (heads, LANES), 1) // ti
    for j in range(tj):
        t, jj = j // groups, j % groups
        turned = pltpu.roll(zb[:, t * LANES : (t + 1) * LANES], lax.rem(grp - jj + groups, groups) * ti, axis=1)
        tile32[pl.ds(j, heads, stride=tj), :] = jnp.where(lane_group == grp, turned, 0.0)
    tsend[...] = tile32[...].reshape(heads, tj, LANES).astype(BF16)

    pl.semaphore_wait(barrier, plane - 1 + len(close))
    for o in (2, -2):
        pl.semaphore_signal(word.at[0], inc=1, device_id=at_z(o), device_id_type=MESH)

    def all_of(ref, n, sem):
        return pltpu.make_async_copy(ref.at[pl.ds(0, n)], ref.at[pl.ds(0, n)], sem)

    def plane_send(src_of, dst, send, recv):
        for place in places:
            samp_id, head_id = at_place(place)
            pltpu.make_async_remote_copy(
                src_ref=src_of(base_of[place[0]] + head_id), dst_ref=dst.at[me_p], send_sem=send, recv_sem=recv,
                device_id=(samp_id, head_id), device_id_type=MESH,
            ).start()

    slot = yh * share + lax.rem(me_h, share)

    def tile_out(h):
        return pltpu.make_async_remote_copy(
            src_ref=tsend.at[h], dst_ref=trecv.at[slot], send_sem=a_send.at[0], recv_sem=a_recv.at[0],
            device_id=(half_of_me * zn + z, h), device_id_type=MESH,
        )

    beside = [place[1:] for place in places if not place[0]]
    for place in beside:
        tile_out(head_at(*place)).start()

    @pl.when(half_of_me == yh)
    def _():
        pltpu.make_async_copy(tsend.at[me_h], trecv.at[slot], a_recv.at[0]).start()

    @pl.when(half_of_me != yh)
    def _():
        tile_out(me_h).start()

    pl.semaphore_wait(word.at[0], 2)
    for o in (4, -4):
        pl.semaphore_signal(word.at[1], inc=1, device_id=at_z(o), device_id_type=MESH)

    for r in range(heads + 1, plane):
        part[r] = jnp.zeros((1, LANES), F32)
    for load in loads[3:]:
        load.wait()
    length = jnp.sum(mask_ref[...].astype(F32), axis=(0, 1), keepdims=True)
    step = 64

    def counting(c, carry):
        ids = lax.broadcasted_iota(jnp.int32, (step, LANES), 0) + (c * step + yh * half)
        acc = jnp.zeros((step, LANES), F32)
        for r in range(atoms // LANES):
            acc = acc + jnp.where(atom_ref[r : r + 1, :] == ids, 1.0, 0.0)
        xs[pl.ds(pl.multiple_of(c * step, step), step), :] = acc
        return carry

    lax.fori_loop(0, half // step, counting, 0)
    counts = dot_nt(jnp.ones((8, LANES), BF16), xs[0:half, :].astype(BF16))[0:1, :]
    real = (lax.broadcasted_iota(jnp.int32, (1, half), 1) + yh * half).astype(F32) < length
    tok = jnp.where(real, counts * (count / atoms), 0.0)
    chunk = LANES // tj
    top[...] = jnp.full(top.shape, -3.0e38, F32)

    def operands(sm):
        if sm:
            query, grad, key, value = qo_ref[...], go_ref[...], ko_ref[...], vo_ref[...]
        else:
            query, grad, key, value = q_ref[yh], g_ref[yh], k_ref[...], v_ref[...]
        return query, (grad.astype(F32) * tok).astype(BF16), key, value

    def raw(sm):
        query, grad, key, value = operands(sm)
        for c in range(tiles):
            cols = slice(c * LANES, (c + 1) * LANES)
            keep = lax.broadcasted_iota(jnp.int32, (LANES, 1), 0).astype(F32) + float(c * LANES) < length
            s = jnp.where(keep, dot_tn(key[:, cols], query) * inv_root, -1000000000.0)
            score[sm, c * chunk : (c + 1) * chunk] = s.reshape(chunk, tj, half)
            dprob[sm, c * chunk : (c + 1) * chunk] = dot_tn(value[:, cols], grad).reshape(chunk, tj, half)

    pltpu.make_async_copy(trecv, trecv, a_recv.at[0]).wait()
    for y in range(YH):
        for t in range(half // LANES):
            block = trecv[y * share + t * groups]
            for u in range(1, groups):
                block = block + trecv[y * share + t * groups + u]
            bias[y, z, :, t * LANES : (t + 1) * LANES] = block

    def ag_copy(sem, y, origin, o):
        return pltpu.make_async_remote_copy(
            src_ref=bias.at[y, wrap(origin)], dst_ref=bias.at[y, wrap(origin)],
            send_sem=ag_send.at[y, sem], recv_sem=ag_recv.at[y, sem], device_id=at_z(o), device_id_type=MESH,
        )

    def absorb(*origins):
        for y in range(YH):
            o = wrap(origins[(y + 1) % len(origins)])
            b = bias[y, o].astype(F32)
            for sm in range(YH):
                s = score[sm, y * zn + o] + b
                score[sm, y * zn + o] = s
                top[sm] = jnp.maximum(top[sm], jnp.max(s.reshape(tj // 8, 8, half), axis=0))

    both = range(YH)

    def put(d, y, origin=0):
        return ag_copy(d + 7, y, origin, origin + d)

    sent = []

    def go(copy):
        copy.start()
        sent.append(copy)

    def pass_on(side):
        for d in (7, 6, 5, 3):
            for y in both:
                go(put(side * d, y, -4 * side))

    def take(*ds):
        for d in ds:
            for y in both:
                put(d, y).wait_recv()
            absorb(-d)

    pl.semaphore_wait(word.at[1], 2)
    for d in (4, -4, 8, 2, -2, 1, -1):
        for y in both:
            go(put(d, y))

    def to_mate(src, dst, i, send, recv):
        return pltpu.make_async_remote_copy(
            src_ref=src, dst_ref=dst, send_sem=send.at[i], recv_sem=recv.at[i], device_id=mate, device_id_type=MESH,
        )

    swaps = [
        to_mate(src, dst, i, x_send, x_recv)
        for i, (src, dst) in enumerate(
            ((q_ref.at[1 - yh], qo_ref), (k_ref, ko_ref), (g_ref.at[1 - yh], go_ref), (v_ref, vo_ref))
        )
    ]
    for swap in swaps:
        go(swap)
    raw(0)
    for side in (1, -1):
        for y in both:
            put(4 * side, y).wait_recv()
        pass_on(side)
    for swap in swaps:
        swap.wait_recv()
    raw(1)
    absorb(0)
    absorb(-4)
    absorb(4)
    take(1, -1, 2, -2, 3, -3, 8, 5, -5, 6, -6, 7, -7)

    largest = [jnp.max(top[sm], axis=0, keepdims=True) for sm in both]

    def first(b, carry):
        new = []
        for sm in both:
            total, dots = carry[2 * sm], carry[2 * sm + 1]
            p = jnp.exp(score[sm, pl.ds(b * 2, 2)] - largest[sm][None])
            score[sm, pl.ds(b * 2, 2)] = p
            pd = p * dprob[sm, pl.ds(b * 2, 2)]
            new.append(total + jnp.sum(p.reshape(2 * tj // 8, 8, half), axis=0))
            new.append(dots + jnp.sum(pd.reshape(2 * tj // 8, 8, half), axis=0))
        return tuple(new)

    zero = jnp.zeros((8, half), F32)
    sums = lax.fori_loop(0, samp // 2, first, (zero,) * 4)
    scale = [1.0 / jnp.sum(sums[2 * sm], axis=0, keepdims=True) for sm in both]
    row_dot = [jnp.sum(sums[2 * sm + 1], axis=0, keepdims=True) * scale[sm] for sm in both]

    def second(b, carry):
        for y in both:
            both_ds = None
            for sm in both:
                prob = score[sm, y * zn + b] * scale[sm]
                probb[sm, y, b] = prob.astype(BF16)
                ds = prob * (dprob[sm, y * zn + b] - row_dot[sm])
                dsb[sm, y, b] = ds.astype(BF16)
                both_ds = ds if sm == 0 else both_ds + ds
            dsum[y, b] = both_ds.astype(BF16)
        return carry

    lax.fori_loop(0, zn, second, 0)

    def rs_copy(sem, y, src, o):
        return pltpu.make_async_remote_copy(
            src_ref=src, dst_ref=rin.at[sem, y], send_sem=rs_send.at[y, sem], recv_sem=rs_recv.at[y, sem],
            device_id=at_z(o), device_id_type=MESH,
        )

    def own(o, y):
        return dsum.at[y, wrap(o)]

    def mine(o, y):
        return dsum[y, wrap(o)].astype(F32)

    def arrived(sem, y):
        rs_copy(sem, y, own(0, y), 1).wait_recv()
        return rin[sem, y].astype(F32)

    def give(d, hop):
        for y in both:
            go(rs_copy(d + 7, y, own(d, y), hop))

    def relay(side):
        for y in both:
            acc = mine(4 * side, y)
            for d in (3, 5, 6, 7):
                acc = acc + arrived(side * d + 7, y)
            racc[(side + 1) // 2, y] = acc.astype(BF16)
            go(rs_copy(4 * side + 7, y, racc.at[(side + 1) // 2, y], 4 * side))

    def rows_out(sm):
        query, grad, key, value = operands(sm)
        attended = dot_nn(value, probb[sm].reshape(count, half)).astype(BF16)
        query_grad = (dot_nn(key, dsb[sm].reshape(count, half)) * inv_root).astype(BF16)
        return attended, query_grad

    def columns_out(sm):
        query, grad, key, value = operands(sm)
        return dot_nt(query, dsb[sm].reshape(count, half)), dot_nt(grad, probb[sm].reshape(count, half))

    for d, hop in ((7, 3), (6, 2), (5, 1), (3, -1)):
        give(d, hop)
        give(-d, -hop)
    for d in (8, 2, -2, 1, -1):
        give(d, d)
    tx_half[0], tx_half[1] = rows_out(1)
    relay(1)
    relay(-1)
    tx_whole[0], tx_whole[1] = columns_out(1)
    results = [
        to_mate(src, dst, i, y_send, y_recv)
        for i, (src, dst) in enumerate(((tx_half, rx_half), (tx_whole, rx_whole)))
    ]
    for result in results:
        go(result)
    att_ref[yh], qg_ref[yh] = rows_out(0)
    key_part, value_part = columns_out(0)
    for y in both:
        acc = mine(0, y)
        for d in (1, -1, 2, -2, 8, 4, -4):
            acc = acc + arrived(d + 7, y)
        for t in range(half // LANES):
            fin[y, t] = acc[:, t * LANES : (t + 1) * LANES].astype(BF16)

    def tile_back(high, x, c):
        spot = col_of[x] + core_of[c]
        return pltpu.make_async_remote_copy(
            src_ref=fin.at[high_of[high], spot // groups], dst_ref=brecv.at[me_h],
            send_sem=b_send.at[0], recv_sem=b_recv.at[0],
            device_id=(samp_of[high], yh * share + spot), device_id_type=MESH,
        )

    for high, lo, x, c in places:
        if not lo:
            tile_back(high, x, c).start()

    @pl.when(half_of_me == yh)
    def _():
        pltpu.make_async_copy(
            fin.at[yh, lax.rem(me_h, share) // groups], brecv.at[me_h], b_recv.at[0]
        ).start()

    @pl.when(half_of_me != yh)
    def _():
        tile_back(0, 0, 0).start()

    pltpu.make_async_copy(brecv, brecv, b_recv.at[0]).wait()
    tile32[...] = brecv[...].astype(F32).reshape(heads * tj, LANES)
    pieces = []
    for t in range(tj // groups):
        piece = jnp.zeros((heads, LANES), F32)
        for jj in range(groups):
            r = tile32[pl.ds(t * groups + jj, heads, stride=tj), :]
            turned = pltpu.roll(r, lax.rem(jj - grp + groups, groups) * ti, axis=1)
            piece = jnp.where(lane_group == jj, turned, piece)
        pieces.append(piece)
    bg = jnp.concatenate(pieces, axis=1)
    hi = bg.astype(BF16)
    lo = (bg - hi.astype(F32)).astype(BF16)
    wpart = dot_nn(hi, ln[...]) + dot_nn(lo, ln[...])
    lng = dot_tn(hi, wt) + dot_tn(lo, wt)
    for r in range(heads):
        part[r] = wpart[r : r + 1, :]
    part[heads] = jnp.sum(lng * norm[...], axis=0, keepdims=True)

    plane_send(lambda p: part.at[p], arr1, s1.at[0], r1.at[0])
    arr1[me_p] = part[me_p]

    for j in range(tj):
        rows = slice(j * ti, (j + 1) * ti)
        n = norm[rows, :]
        dn = lng[rows, :] * gain
        out = dn - jnp.mean(dn, axis=-1, keepdims=True) - n * jnp.mean(dn * n, axis=-1, keepdims=True)
        xs[pl.ds(j, ti, stride=tj), :] = out * inv[rows, :]
    pg_ref[...] = xs[...].reshape(ti, tj, LANES).astype(BF16)

    for result in results:
        result.wait_recv()
    att_ref[1 - yh] = rx_half[0]
    qg_ref[1 - yh] = rx_half[1]
    kg_ref[...] = ((key_part + rx_whole[0]) * inv_root).astype(BF16)
    vg_ref[...] = (value_part + rx_whole[1]).astype(BF16)
    all_of(trecv, heads - 1, a_send.at[0]).wait()
    all_of(brecv, heads - 1, b_send.at[0]).wait()

    @pl.when(half_of_me != yh)
    def _():
        all_of(trecv, 1, a_send.at[0]).wait()
        all_of(brecv, 1, b_send.at[0]).wait()

    for copy in sent:
        copy.wait_send()
    all_of(arr1, plane - 1, r1.at[0]).wait()
    row[...] = jnp.sum(arr1[...], axis=0)

    for off in sorted(range(1, zn), key=lambda o: -min(o, zn - o)):
        pltpu.make_async_remote_copy(
            src_ref=row, dst_ref=arr2.at[z], send_sem=s2.at[0], recv_sem=r2.at[0],
            device_id=at_z(off), device_id_type=MESH,
        ).start()
    arr2[z] = row[...]
    all_of(arr2, zn - 1, r2.at[0]).wait()
    tot[...] = jnp.sum(arr2[...], axis=0) * (1.0 / count)
    plane_send(lambda p: tot, res, s3.at[0], r3.at[0])
    res[me_p] = tot[...]
    all_of(res, plane - 1, r3.at[0]).wait()
    wg_ref[...] = jnp.concatenate([res[r] for r in range(heads)], axis=0)
    gg_ref[...] = res[heads]

    all_of(arr1, plane - 1, s1.at[0]).wait()
    all_of(arr2, zn - 1, s2.at[0]).wait()
    all_of(res, plane - 1, s3.at[0]).wait()


def put_out(*refs):
    sem = refs[-1]
    half = refs[0].shape[2]
    pairs = [(refs[i].at[y], refs[7 + i].at[:, y * half : (y + 1) * half]) for i in range(2) for y in range(YH)]
    pairs += [(refs[i], refs[7 + i]) for i in range(2, 7)]
    copies = [pltpu.make_async_copy(src, dst, sem.at[i]) for i, (src, dst) in enumerate(pairs)]
    for copy in copies:
        copy.start()
    for copy in copies:
        copy.wait()


def local(samp, heads, queries, keys, values, out_grad, pair, ln_gain, proj_weight, token_mask, atom_map):
    _, feat, count = queries.shape
    ti, tj, chan = pair.shape
    atoms = atom_map.shape[0]
    zn = samp // YH
    plane = YH * heads
    tiles = count // LANES
    vmem = pl.BlockSpec(memory_space=pltpu.VMEM)
    row = (1, LANES)
    dma = pltpu.SemaphoreType.DMA
    operands = (
        pair, ln_gain.reshape(1, chan), proj_weight.T, token_mask.reshape(tiles, LANES),
        atom_map.reshape(atoms // LANES, LANES), out_grad[0], queries[0], keys[0], values[0],
    )
    half = count // YH
    halves = ((YH, feat, half), BF16)
    wide = ((feat, count), BF16)
    loaded = [(x.shape, x.dtype) for x in operands[:5]] + [halves, halves, wide, wide]
    loaded += [wide, wide, ((feat, half), BF16), ((feat, half), BF16)]
    scratch = [pltpu.VMEM(*x) for x in loaded] + [
        pltpu.VMEM((max(ti * tj, count), LANES), F32),
        pltpu.VMEM((ti * tj, LANES), F32),
        pltpu.VMEM((ti * tj, LANES), F32),
        pltpu.VMEM((ti * tj, LANES), BF16),
        pltpu.VMEM((heads * tj, LANES), F32),
        pltpu.VMEM((heads, tj, LANES), BF16),
        pltpu.VMEM((heads, tj, LANES), BF16),
        pltpu.VMEM((YH, zn, tj, half), BF16),
        pltpu.VMEM((YH, samp, tj, half), F32),
        pltpu.VMEM((YH, samp, tj, half), F32),
        pltpu.VMEM((YH, YH, zn, tj, half), BF16),
        pltpu.VMEM((YH, YH, zn, tj, half), BF16),
        pltpu.VMEM((YH, zn, tj, half), BF16),
        pltpu.VMEM((YH, 8, half), F32),
        pltpu.VMEM((2, feat, half), BF16),
        pltpu.VMEM((2, feat, half), BF16),
        pltpu.VMEM((2, feat, count), F32),
        pltpu.VMEM((2, feat, count), F32),
        pltpu.VMEM((16, YH, tj, half), BF16),
        pltpu.VMEM((2, YH, tj, half), BF16),
        pltpu.VMEM((YH, half // LANES, tj, LANES), BF16),
        pltpu.VMEM((heads, tj, LANES), BF16),
        pltpu.VMEM((plane,) + row, F32),
        pltpu.VMEM((plane,) + row, F32),
        pltpu.VMEM(row, F32),
        pltpu.VMEM((zn,) + row, F32),
        pltpu.VMEM(row, F32),
        pltpu.VMEM((plane,) + row, F32),
        dma((1,)), dma((1,)), dma((YH, 16)), dma((YH, 16)), dma((YH, 16)), dma((YH, 16)),
        dma((1,)), dma((1,)), dma((1,)), dma((1,)), dma((1,)), dma((1,)), dma((1,)), dma((1,)), dma((4,)), dma((4,)), dma((2,)), dma((2,)), dma((11,)), pltpu.SemaphoreType.REGULAR((2,)),
    ]
    shape = jax.ShapeDtypeStruct
    tail = (
        shape((feat, count), BF16), shape((feat, count), BF16), shape((ti, tj, chan), BF16),
        shape((heads, chan), F32), shape((1, chan), F32),
    )
    outs = (shape((feat, count), BF16),) * 2 + tail
    hbm = pl.BlockSpec(memory_space=pltpu.HBM)
    results = pl.pallas_call(
        functools.partial(kernel, samp, heads, atoms),
        out_shape=(shape((YH, feat, half), BF16),) * 2 + tail,
        in_specs=[hbm] * 9,
        out_specs=(vmem,) * 7,
        scratch_shapes=scratch,
        compiler_params=pltpu.CompilerParams(
            collective_id=0, has_side_effects=True, vmem_limit_bytes=48 * 1024 * 1024
        ),
    )(*(pltpu.with_memory_space_constraint(x, pltpu.HBM) for x in operands))
    att, qg, kg, vg, pg, wg, gg = pl.pallas_call(
        put_out,
        out_shape=outs,
        in_specs=[vmem] * 7,
        out_specs=(hbm,) * 7,
        scratch_shapes=[dma((9,))],
        compiler_params=pltpu.CompilerParams(vmem_limit_bytes=16 * 1024 * 1024),
    )(*results)
    return att[None], qg[None], kg[None], vg[None], pg, wg.T, gg[0]


def solution(mesh):
    cut = P("samp", "head", None)
    return jax.shard_map(
        functools.partial(local, mesh.shape["samp"], mesh.shape["head"]),
        mesh=mesh,
        in_specs=(cut, cut, cut, cut, P("head", "samp", None), P(), P(), P(), P()),
        out_specs=(cut, cut, cut, cut, P("head", "samp", None), P(), P()),
        check_vma=False,
    )
```
